32 devices in a mesh: ctx: 16 (over z, x, core), head: 2 (over y).
Axes of the slice: x: 2, y: 2, z: 4, core: 2. Of those that a mesh axis runs over, the one named last changes fastest.
Arguments:
- queries: bfloat16 [16384, 1024], P(('ctx', 'head'))
- keys: bfloat16 [16384, 256], P(('ctx', 'head'))
- values: bfloat16 [16384, 256], P(('ctx', 'head')), may hold values from -6 to 6
- q_feature: bfloat16 [8, 128, 64], P('head'), may hold values from -0.5 to 0.5
- k_feature: bfloat16 [2, 128, 64], P('head'), may hold values from -0.5 to 0.5
- doc_lengths: int32 [64], replicated, may hold values from 1 to 7680, as said below
Outputs:
- attended: bfloat16 [16384, 1024], P('ctx', 'head')
The draws below stay inside these ranges and needn't reach their ends.
Inputs may be any that keep to these rules, and one draw needn't show every extreme that they name: `doc_lengths`: positive lengths that sum to 16384; the first document has length 7680 and the second 3 * 1024.
All inputs are finite; a program needn't handle non-finite values.
Results may differ from the reference program's by a relative error of at most 0.0052.
Values may be sent and summed in bfloat16 or wider, within the bound.
A program may use at most 64 MiB of HBM per device.

```python
import jax
import jax.numpy as jnp
from jax import lax

HD = 128
HALF = 64
T_CTX = 1024
DOCS = 64
KVH = 2
QH = 8
TOKENS = 16384


def draw_queries(key, part):
    shape = (TOKENS, QH * HD)
    base = jnp.clip(jax.random.normal(jax.random.fold_in(key, 1), shape, jnp.float32), -6.0, 6.0)
    return base.astype(jnp.bfloat16)


def draw_keys(key, part):
    shape = (TOKENS, KVH * HD)
    base = jnp.clip(jax.random.normal(jax.random.fold_in(key, 5), shape, jnp.float32), -6.0, 6.0)
    return base.astype(jnp.bfloat16)


def draw_doc_lengths(key, part):
    first_length = TOKENS // 2 - T_CTX // 2
    second_length = 3 * T_CTX
    rest_total = TOKENS - first_length - second_length
    shuffled = jax.random.permutation(jax.random.fold_in(key, 11), rest_total - 1).astype(jnp.int32) + 1
    cut_points = jnp.sort(shuffled[:DOCS - 3])
    bounds = jnp.concatenate([jnp.zeros((1,), jnp.int32), cut_points, jnp.full((1,), rest_total, jnp.int32)])
    rest_lengths = (bounds[1:] - bounds[:-1]).astype(jnp.int32)
    return jnp.concatenate([jnp.full((1,), first_length, jnp.int32), jnp.full((1,), second_length, jnp.int32), rest_lengths]).astype(jnp.int32)


def levels(key, shape, split, smallest, largest):
    loudness, own = 1.0, jax.random.fold_in(key, 6)
    for position, shards_of in split:
        heights = jnp.exp(jax.random.uniform(jax.random.fold_in(own, position), (shards_of,), jnp.float32, smallest / len(split), largest / len(split)))
        loudness = loudness * jnp.repeat(heights, shape[position] // shards_of).reshape([-1 if axis == position else 1 for axis in range(len(shape))])
    return loudness


def scatter_about(rng, dims, scale, bound, cuts=(), held_as=jnp.bfloat16):
    values = scale * jax.random.normal(rng, dims, jnp.float32)
    if cuts:
        values = values * levels(rng, dims, cuts, -0.22, 0.18)
    return jnp.clip(values, -bound, bound).astype(held_as)


def setup_inputs(seed: int = 0) -> dict:
    key_of = jax.random.split(jax.random.key(seed), 7)
    queries = draw_queries(jax.random.fold_in(key_of[6], 71), 0)
    keys = draw_keys(jax.random.fold_in(key_of[6], 71), 0)
    values = scatter_about(key_of[2], (TOKENS, KVH * HD), 1.0, 6.0, ((0, 32),))
    q_feature = scatter_about(key_of[3], (QH, HD, HALF), HD ** -0.5, 0.5, ((0, 2),))
    k_feature = scatter_about(key_of[4], (KVH, HD, HALF), HD ** -0.5, 0.5, ((0, 2),))
    doc_lengths = draw_doc_lengths(jax.random.fold_in(key_of[6], 71), 0)
    return dict(queries=queries, keys=keys, values=values, q_feature=q_feature, k_feature=k_feature, doc_lengths=doc_lengths)


def hedgehog(inputs, weight):
    projected = jnp.einsum("nhd,hdf->nhf", inputs.astype(jnp.float32), weight.astype(jnp.float32))
    return jnp.concatenate([jax.nn.softmax(projected, -1), jax.nn.softmax(-projected, -1)], -1).astype(jnp.bfloat16)


def block_state(phi_k, values, doc_ids):
    last_mask = (doc_ids == doc_ids[-1]).astype(jnp.bfloat16)[:, None]
    chosen = phi_k * last_mask
    state_s = jnp.dot(chosen.T, values, preferred_element_type=jnp.float32)
    state_z = jnp.sum(chosen.astype(jnp.float32), 0)
    return state_s, state_z


def block_output(phi_q, phi_k, values, doc_ids, prev_doc, carry_s, carry_z):
    length = doc_ids.shape[0]
    rows_index = jnp.arange(length)
    causal = (rows_index[None, :] <= rows_index[:, None]) & (doc_ids[:, None] == doc_ids[None, :])
    carried = (doc_ids == prev_doc).astype(jnp.float32)
    results = []
    for head_index in range(phi_q.shape[1]):
        phi_head = phi_q[:, head_index, :]
        scores = jnp.dot(phi_head, phi_k.T, preferred_element_type=jnp.float32)
        masked = jnp.where(causal, scores, 0.0)
        wide_head = phi_head.astype(jnp.float32)
        denominator = jnp.sum(masked, -1) + carried * jnp.dot(wide_head, carry_z, precision=lax.Precision.HIGHEST)
        numerator = jnp.dot(masked.astype(jnp.bfloat16), values, preferred_element_type=jnp.float32)
        numerator = numerator + carried[:, None] * jnp.dot(wide_head, carry_s, precision=lax.Precision.HIGHEST)
        results.append(numerator / denominator[:, None])
    return jnp.stack(results, 1)


def reference(queries, keys, values, q_feature, k_feature, doc_lengths):
    starts = jnp.cumsum(doc_lengths) - doc_lengths
    blocks = TOKENS // T_CTX
    head_size = q_feature.shape[1]
    kv_heads = k_feature.shape[0]
    per_group = q_feature.shape[0] // kv_heads
    feats = 2 * q_feature.shape[2]
    q_blocks = queries.reshape(blocks, T_CTX, -1, head_size)
    k_blocks = keys.reshape(blocks, T_CTX, kv_heads, head_size)
    v_blocks = values.reshape(blocks, T_CTX, kv_heads, head_size)

    def advance(totals, inputs):
        q_here, k_here, v_here, block_index = inputs
        begin = block_index * T_CTX
        positions = begin + jnp.arange(T_CTX).astype(jnp.int32)
        doc_ids = (jnp.sum((starts[None, :] <= positions[:, None]).astype(jnp.int32), 1) - 1).astype(jnp.int32)
        prev_doc = (jnp.sum((starts <= begin - 1).astype(jnp.int32)) - 1).astype(jnp.int32)
        phi_q = hedgehog(q_here, q_feature).reshape(T_CTX, kv_heads, per_group, feats).transpose(1, 0, 2, 3)
        phi_k = hedgehog(k_here, k_feature).transpose(1, 0, 2)
        vals_heads = v_here.transpose(1, 0, 2)
        outputs = jax.vmap(block_output, in_axes=(0, 0, 0, None, None, 0, 0))(phi_q, phi_k, vals_heads, doc_ids, prev_doc, totals[0], totals[1])
        state_s, state_z = jax.vmap(block_state, in_axes=(0, 0, None))(phi_k, vals_heads, doc_ids)
        keep = 1.0 - (doc_ids[-1] != prev_doc).astype(jnp.float32)
        new_totals = (state_s + keep * totals[0], state_z + keep * totals[1])
        return new_totals, outputs.transpose(1, 0, 2, 3).reshape(T_CTX, -1).astype(jnp.bfloat16)

    initial = (jnp.zeros((kv_heads, feats, head_size), jnp.float32), jnp.zeros((kv_heads, feats), jnp.float32))
    indices = jnp.arange(blocks).astype(jnp.int32)
    finals, outputs = lax.scan(advance, initial, (q_blocks, k_blocks, v_blocks, indices))
    return outputs.reshape(TOKENS, -1)
```

```python
import functools

import jax
import jax.numpy as jnp
from jax import lax
from jax.experimental import pallas as pl
from jax.experimental.pallas import tpu as pltpu
from jax.sharding import PartitionSpec as P

MESH = pl.DeviceIdType.MESH
F32 = jnp.float32
BF16 = jnp.bfloat16
NT = (((1,), (1,)), ((), ()))
SECOND = 3 * 1024
ZROWS = 16
BLOCK = 128
SPAN = 80.0


def iota(shape, dim):
    return lax.broadcasted_iota(jnp.int32, shape, dim)


def extremes(p):
    return jnp.max(p, 0, keepdims=True), jnp.min(p, 0, keepdims=True)


def features(p):
    top, low = extremes(p)
    up, down = jnp.exp(p - top), jnp.exp(low - p)
    up = up * (1.0 / jnp.sum(up, 0, keepdims=True))
    down = down * (1.0 / jnp.sum(down, 0, keepdims=True))
    return jnp.concatenate([up, down], 0)


def encode(p):
    top, low = extremes(p)
    reach = jnp.minimum(SPAN, 0.5 * (top - low))
    return jnp.exp(jnp.maximum(p - top + reach, 0.0) + jnp.minimum(p - low - reach, 0.0)).astype(BF16)


def decode(u):
    up = u.astype(F32)
    down = 1.0 / up
    up = up * (1.0 / jnp.sum(up, 0, keepdims=True))
    down = down * (1.0 / jnp.sum(down, 0, keepdims=True))
    return jnp.concatenate([up, down], 0)


def kernel(
    n_ctx, n_head, n0, n1, reach,
    q_hbm, k_hbm, v_hbm, wq_hbm, wk_hbm, len_hbm, out_ref,
    xq, xk, v_buf, wq_buf, wk_buf, len_ref,
    uk_out, uq_out, uk_in, uq_in, phi_k, v_ext, phi_q, held, carry, lo_ref, state_out, state_in,
    load_sem, w_send, w_recv, kv_send, kv_recv, q_send, q_recv, s_send, s_recv,
    here_sem, all_sem, ctx_sem,
):
    me, b = lax.axis_index("head"), lax.axis_index("ctx")
    rows, hd = q_hbm.shape[0], BLOCK
    heads = wq_hbm.shape[0]
    half = hd // 2
    wide = heads * hd
    blocks = phi_k.shape[0]
    per = rows // BLOCK
    step = min(2, per)
    length = blocks * BLOCK
    begin = b * length
    others = range(1, n_head)

    def peer(o):
        return lax.rem(me + o, n_head)

    def last_of(j):
        return jnp.where(j < n0, n0 - 1, jnp.where(j < n1, n1 - 1, n_ctx - 1))

    def first_of(j):
        return jnp.where(j < n0, 0, jnp.where(j < n1, n0, n1))

    n_to = jnp.minimum(last_of(b) + 1, n_ctx - 1) - b
    n_from = jnp.where(b == 0, 0, b - first_of(b - 1))

    barrier = pltpu.get_barrier_semaphore()

    @pl.when(me == 0)
    def _():
        for o in others:
            pl.semaphore_signal(barrier, inc=1, device_id=(b, o), device_id_type=MESH)

    own = pl.ds(pl.multiple_of(me * rows, rows), rows)

    def q_cols(o):
        return pl.ds(pl.multiple_of(peer(o) * wide, wide), wide)

    def kv_cols(o):
        return pl.ds(pl.multiple_of(peer(o) * hd, hd), hd)

    small = [
        pltpu.make_async_copy(src, dst, load_sem.at[i])
        for i, (src, dst) in enumerate(
            ((len_hbm, len_ref), (wk_hbm, wk_buf.at[0]), (wq_hbm, wq_buf.at[0]))
        )
    ]
    k_load = [
        pltpu.make_async_copy(k_hbm.at[:, kv_cols(o)], xk.at[o], load_sem.at[4 + o])
        for o in range(n_head)
    ]
    v_load = pltpu.make_async_copy(v_hbm.at[:, kv_cols(0)], v_buf.at[own, :], load_sem.at[3])
    q_load = [
        pltpu.make_async_copy(q_hbm.at[:, q_cols(o)], xq.at[o], load_sem.at[4 + n_head + o])
        for o in range(n_head)
    ]
    for c in (*small, *k_load, v_load, *q_load):
        c.start()

    @pl.when(me != 0)
    def _():
        pl.semaphore_wait(barrier, 1)
        pl.semaphore_signal(here_sem, inc=1, device_id=(b, 0), device_id_type=MESH)

    @pl.when(me == 0)
    def _():
        pl.semaphore_wait(here_sem, n_head - 1)

    if n_head > 2:

        @pl.when(me == 0)
        def _():
            for o in others:
                pl.semaphore_signal(all_sem, inc=1, device_id=(b, o), device_id_type=MESH)

        @pl.when(me != 0)
        def _():
            pl.semaphore_wait(all_sem, 1)

    def remote(src, dst, send, recv, o):
        return pltpu.make_async_remote_copy(
            src_ref=src, dst_ref=dst, send_sem=send, recv_sem=recv,
            device_id=(b, peer(o)), device_id_type=MESH,
        )

    def w_copy(o, which):
        src, dst = ((wk_hbm, wk_buf), (wq_hbm, wq_buf))[which]
        slot = n_head - o
        return remote(
            src, dst.at[slot], w_send.at[slot - 1, which], w_recv.at[slot - 1, which], o
        )

    def v_copy(o):
        slot = n_head - o - 1
        return remote(
            v_hbm.at[:, kv_cols(o)], v_buf.at[own, :], kv_send.at[slot, 0], kv_recv.at[slot, 0], o
        )

    def k_copy(o):
        slot = n_head - o - 1
        return remote(
            uk_out.at[slot], uk_in.at[slot], kv_send.at[slot, 1], kv_recv.at[slot, 1], o
        )

    def q_copy(o, i):
        slot = n_head - o - 1
        return remote(
            uq_out.at[slot, i], uq_in.at[slot, i], q_send.at[slot, i], q_recv.at[slot, i], o
        )

    for o in others:
        w_copy(o, 0).start()
        w_copy(o, 1).start()
    for o in others:
        v_copy(o).start()

    @pl.when(me == 0)
    def _():
        def greet(i, _):
            @pl.when(i <= n_to)
            def _():
                pl.semaphore_signal(barrier, inc=1, device_id=(b + i, 0), device_id_type=MESH)

            @pl.when(i <= n_from)
            def _():
                pl.semaphore_signal(barrier, inc=1, device_id=(b - i, 0), device_id_type=MESH)

            return 0

        lax.fori_loop(1, reach + 1, greet, 0)

    for c in small:
        c.wait()
    docs = len_ref.shape[1]
    lens = jnp.broadcast_to(len_ref[...].astype(F32), (docs, docs))
    starts = jnp.sum(
        jnp.where(iota((docs, docs), 1) < iota((docs, docs), 0), lens, 0.0), 1, keepdims=True
    )

    def doc_start(pos):
        return jnp.max(jnp.where(starts <= pos, starts, -1.0), 0, keepdims=True)

    lane = iota((1, BLOCK), 1)
    for c in range(blocks):
        pos = (begin + c * BLOCK + lane).astype(F32)
        lo_ref[c] = jnp.broadcast_to(doc_start(pos), (8, BLOCK))
    v_ext[:, hd:, :] = jnp.ones((blocks, ZROWS, BLOCK), BF16)

    def pair_weights(o):
        zero = jnp.zeros((half, hd), BF16)
        return [
            jnp.concatenate(
                [
                    jnp.concatenate([wq_buf[o, h], zero], 1),
                    jnp.concatenate([zero, wq_buf[o, h + 1]], 1),
                ],
                0,
            )
            for h in range(0, heads, 2)
        ]

    def token_rows(i, n=1):
        return pl.ds(pl.multiple_of(i * BLOCK, BLOCK), n * BLOCK)

    def set_keys(c, phi):
        phi_k[c] = phi.T.astype(BF16)
        v_ext[c, :hd, :] = v_buf[token_rows(c), :].T

    k_load[0].wait()
    v_load.wait()

    def own_keys(i, _):
        p = lax.dot_general(
            wk_buf[0], xk[0, token_rows(i * step, step), :], NT, preferred_element_type=F32
        )
        phi = features(p)
        for j in range(step):
            set_keys(me * per + i * step + j, phi[:, j * BLOCK : (j + 1) * BLOCK])
        return 0

    lax.fori_loop(0, per // step, own_keys, 0)
    q_load[0].wait()
    weights = pair_weights(0)

    def own_queries(i, _):
        for n, w in enumerate(weights):
            x = xq[0, token_rows(i * step, step), 2 * n * hd : 2 * (n + 1) * hd]
            p = lax.dot_general(w, x, NT, preferred_element_type=F32)
            for m in range(2):
                phi = features(p[m * half : (m + 1) * half]).astype(BF16)
                h = 2 * n + m
                for j in range(step):
                    phi_q[me * per + i * step + j, :, h * hd : (h + 1) * hd] = phi[
                        :, j * BLOCK : (j + 1) * BLOCK
                    ]
        return 0

    lax.fori_loop(0, per // step, own_queries, 0)

    for o in others:
        w_copy(n_head - o, 0).wait_recv()
        k_load[o].wait()
        p = lax.dot_general(wk_buf[o], xk[o], NT, preferred_element_type=F32)
        uk_out[n_head - o - 1] = encode(p)
        k_copy(o).start()
    for o in others:
        w_copy(n_head - o, 1).wait_recv()
        q_load[o].wait()
        weights = pair_weights(o)
        for i in range(per // step):
            for n, w in enumerate(weights):
                x = xq[o, token_rows(i * step, step), 2 * n * hd : 2 * (n + 1) * hd]
                p = lax.dot_general(w, x, NT, preferred_element_type=F32)
                for m in range(2):
                    u = encode(p[m * half : (m + 1) * half])
                    h = 2 * n + m
                    for j in range(step):
                        uq_out[n_head - o - 1, i * step + j, h * half : (h + 1) * half, :] = u[
                            :, j * BLOCK : (j + 1) * BLOCK
                        ]
            for j in range(step):
                q_copy(o, i * step + j).start()

    for o in others:
        v_copy(n_head - o).wait_recv()
        k_copy(n_head - o).wait_recv()
        phi = decode(uk_in[o - 1])
        for i in range(per):
            set_keys(peer(o) * per + i, phi[:, i * BLOCK : (i + 1) * BLOCK])

    total = jnp.zeros((hd + ZROWS, hd), F32)
    for c in range(blocks):
        carry[c] = total
        c0 = begin + c * BLOCK
        edge = doc_start((c0 + BLOCK - 1).astype(F32))
        chosen = ((c0 + lane).astype(F32) >= edge).astype(F32).astype(BF16)
        new = jnp.dot(v_ext[c] * chosen, phi_k[c], preferred_element_type=F32)
        total = new + jnp.where(edge < c0.astype(F32), total, 0.0)
    state_out[...] = total.astype(BF16)

    @pl.when(me == 0)
    def _():
        pl.semaphore_wait(barrier, n_to + n_from)
        for o in others:
            pl.semaphore_signal(ctx_sem, inc=1, device_id=(b, o), device_id_type=MESH)

    @pl.when(me != 0)
    def _():
        pl.semaphore_wait(ctx_sem, 1)

    def s_copy(i):
        return pltpu.make_async_remote_copy(
            src_ref=state_out,
            dst_ref=state_in.at[i - 1],
            send_sem=s_send.at[i - 1],
            recv_sem=s_recv.at[i - 1],
            device_id=(b + i, me),
            device_id_type=MESH,
        )

    def push(i, _):
        @pl.when(i <= n_to)
        def _():
            s_copy(i).start()

        return 0

    lax.fori_loop(1, reach + 1, push, 0)

    before = doc_start((begin - 1).astype(F32))
    carry[blocks] = jnp.zeros((hd + ZROWS, hd), F32)

    def collect(i, _):
        @pl.when(i <= n_from)
        def _():
            s_copy(i).wait_recv()
            end = ((b - i + 1) * length - 1).astype(F32)
            carry[blocks] += jnp.where(end >= before, state_in[i - 1].astype(F32), 0.0)

        return 0

    lax.fori_loop(1, reach + 1, collect, 0)
    for c in range(blocks):
        edge = doc_start((begin + c * BLOCK - 1).astype(F32))
        entering = jnp.where(edge < begin.astype(F32), carry[blocks], 0.0)
        held[c] = (carry[c] + entering).astype(BF16)

    def attend(c):
        c0 = begin + c * BLOCK
        q = phi_q[c]
        scores = jnp.dot(phi_k[c], q, preferred_element_type=F32)
        lo = lo_ref[c, 0:1, :]
        s_i = iota((BLOCK, BLOCK), 0)
        mask = (s_i <= iota((BLOCK, BLOCK), 1)) & ((c0 + s_i).astype(F32) >= lo)
        carried = (lo < c0.astype(F32)).astype(F32).astype(BF16)
        parts = [
            jnp.where(mask, scores[:, h * hd : (h + 1) * hd], 0.0).astype(BF16)
            for h in range(heads)
        ]
        old = q * jnp.concatenate([carried] * heads, 1)
        left = jnp.concatenate([v_ext[c], held[c]], 1)
        right = jnp.concatenate([jnp.concatenate(parts, 1), old], 0)
        acc = jnp.dot(left, right, preferred_element_type=F32)
        out = acc[:hd] * (1.0 / acc[hd : hd + 1])
        for h in range(heads):
            out_ref[token_rows(c), h * hd : (h + 1) * hd] = out[:, h * hd : (h + 1) * hd].T.astype(
                BF16
            )

    def own_block(i, _):
        attend(me * per + i)
        return 0

    lax.fori_loop(0, per, own_block, 0)
    for o in others:
        first = peer(o) * per

        def peer_block(i, _):
            q_copy(n_head - o, i).wait_recv()
            for h in range(heads):
                phi_q[first + i, :, h * hd : (h + 1) * hd] = decode(
                    uq_in[o - 1, i, h * half : (h + 1) * half, :]
                ).astype(BF16)
            attend(first + i)
            return 0

        lax.fori_loop(0, per, peer_block, 0)

    for o in others:
        w_copy(o, 0).wait_send()
        w_copy(o, 1).wait_send()
        v_copy(o).wait_send()
        k_copy(o).wait_send()
        for i in range(per):
            q_copy(o, i).wait_send()

    def pushed(i, _):
        @pl.when(i <= n_to)
        def _():
            s_copy(i).wait_send()

        return 0

    lax.fori_loop(1, reach + 1, pushed, 0)


def body(n_ctx, n_head, queries, keys, values, q_feature, k_feature, doc_lengths):
    rows = queries.shape[0]
    heads, hd, half = q_feature.shape
    length = rows * n_head
    tokens = length * n_ctx
    blocks = length // BLOCK
    per = rows // BLOCK
    first = tokens // 2 - length // 2
    n0, n1 = first // length, (first + SECOND) // length
    reach = min(max(n0, n1 - n0, n_ctx - n1), n_ctx - 1)
    hbm = pl.BlockSpec(memory_space=pltpu.HBM)
    vmem = pl.BlockSpec(memory_space=pltpu.VMEM)
    dma, plain = pltpu.SemaphoreType.DMA, pltpu.SemaphoreType.REGULAR
    others = max(n_head - 1, 1)
    operands = (
        queries, keys, values,
        q_feature.transpose(0, 2, 1), k_feature[0].T,
        doc_lengths.reshape(1, -1),
    )
    return pl.pallas_call(
        functools.partial(kernel, n_ctx, n_head, n0, n1, reach),
        out_shape=jax.ShapeDtypeStruct((length, heads * hd), BF16),
        in_specs=[hbm] * 6,
        out_specs=vmem,
        scratch_shapes=[
            pltpu.VMEM((n_head, rows, heads * hd), BF16),
            pltpu.VMEM((n_head, rows, hd), BF16),
            pltpu.VMEM((length, hd), BF16),
            pltpu.VMEM((n_head, heads, half, hd), BF16),
            pltpu.VMEM((n_head, half, hd), BF16),
            pltpu.VMEM((1, doc_lengths.shape[0]), jnp.int32),
            pltpu.VMEM((others, half, rows), BF16),
            pltpu.VMEM((others, per, heads * half, BLOCK), BF16),
            pltpu.VMEM((others, half, rows), BF16),
            pltpu.VMEM((others, per, heads * half, BLOCK), BF16),
            pltpu.VMEM((blocks, BLOCK, 2 * half), BF16),
            pltpu.VMEM((blocks, hd + ZROWS, BLOCK), BF16),
            pltpu.VMEM((blocks, 2 * half, heads * BLOCK), BF16),
            pltpu.VMEM((blocks, hd + ZROWS, 2 * half), BF16),
            pltpu.VMEM((blocks + 1, hd + ZROWS, 2 * half), F32),
            pltpu.VMEM((blocks, 8, BLOCK), F32),
            pltpu.VMEM((hd + ZROWS, 2 * half), BF16),
            pltpu.VMEM((reach, hd + ZROWS, 2 * half), BF16),
            dma((4 + 2 * n_head,)),
            dma((others, 2)),
            dma((others, 2)),
            dma((others, 2)),
            dma((others, 2)),
            dma((others, per)),
            dma((others, per)),
            dma((reach,)),
            dma((reach,)),
            plain, plain, plain,
        ],
        compiler_params=pltpu.CompilerParams(
            collective_id=0, has_side_effects=True, vmem_limit_bytes=32 << 20
        ),
    )(*[pltpu.with_memory_space_constraint(a, pltpu.HBM) for a in operands])


def solution(mesh):
    placed = (
        P(("ctx", "head"), None),
        P(("ctx", "head"), None),
        P(("ctx", "head"), None),
        P("head", None, None),
        P("head", None, None),
        P(),
    )
    return jax.shard_map(
        functools.partial(body, mesh.shape["ctx"], mesh.shape["head"]),
        mesh=mesh,
        in_specs=placed,
        out_specs=P("ctx", "head"),
        check_vma=False,
    )
```

```python
import functools

import jax
import jax.numpy as jnp
from jax import lax
from jax.experimental import pallas as pl
from jax.experimental.pallas import tpu as pltpu
from jax.sharding import PartitionSpec as P

MESH = pl.DeviceIdType.MESH
F32 = jnp.float32
BF16 = jnp.bfloat16
NT = (((1,), (1,)), ((), ()))
SECOND = 3 * 1024
ZROWS = 16
BLOCK = 128
SPAN = 80.0


def iota(shape, dim):
    return lax.broadcasted_iota(jnp.int32, shape, dim)


def extremes(p):
    return jnp.max(p, 0, keepdims=True), jnp.min(p, 0, keepdims=True)


def features(p):
    top, low = extremes(p)
    up, down = jnp.exp(p - top), jnp.exp(low - p)
    up = up * (1.0 / jnp.sum(up, 0, keepdims=True))
    down = down * (1.0 / jnp.sum(down, 0, keepdims=True))
    return jnp.concatenate([up, down], 0)


def encode(p):
    top, low = extremes(p)
    reach = jnp.minimum(SPAN, 0.5 * (top - low))
    return jnp.exp(jnp.maximum(p - top + reach, 0.0) + jnp.minimum(p - low - reach, 0.0)).astype(BF16)


def decode(u):
    up = u.astype(F32)
    down = 1.0 / up
    up = up * (1.0 / jnp.sum(up, 0, keepdims=True))
    down = down * (1.0 / jnp.sum(down, 0, keepdims=True))
    return jnp.concatenate([up, down], 0)


def kernel(
    n_ctx, n_head, n0, n1, reach,
    q_hbm, k_hbm, v_hbm, wq_hbm, wk_hbm, len_hbm, out_ref,
    xq, xk, v_buf, wq_buf, wk_buf, len_ref,
    uk_out, uq_out, uk_in, uq_in, phi_k, v_ext, phi_q, held, carry, fresh, lo_ref, state_out, state_in,
    load_sem, w_send, w_recv, kv_send, kv_recv, q_send, q_recv, s_send, s_recv,
    here_sem, all_sem, ctx_sem,
):
    me, b = lax.axis_index("head"), lax.axis_index("ctx")
    rows, hd = q_hbm.shape[0], BLOCK
    heads = wq_hbm.shape[0]
    half = hd // 2
    wide = heads * hd
    blocks = phi_k.shape[0]
    per = rows // BLOCK
    step = min(2, per)
    length = blocks * BLOCK
    begin = b * length
    others = range(1, n_head)

    def peer(o):
        return lax.rem(me + o, n_head)

    def last_of(j):
        return jnp.where(j < n0, n0 - 1, jnp.where(j < n1, n1 - 1, n_ctx - 1))

    def first_of(j):
        return jnp.where(j < n0, 0, jnp.where(j < n1, n0, n1))

    n_to = jnp.minimum(last_of(b) + 1, n_ctx - 1) - b
    n_from = jnp.where(b == 0, 0, b - first_of(b - 1))

    barrier = pltpu.get_barrier_semaphore()

    @pl.when(me == 0)
    def _():
        for o in others:
            pl.semaphore_signal(barrier, inc=1, device_id=(b, o), device_id_type=MESH)

    own = pl.ds(pl.multiple_of(me * rows, rows), rows)

    def q_cols(o):
        return pl.ds(pl.multiple_of(peer(o) * wide, wide), wide)

    def kv_cols(o):
        return pl.ds(pl.multiple_of(peer(o) * hd, hd), hd)

    small = [
        pltpu.make_async_copy(src, dst, load_sem.at[i])
        for i, (src, dst) in enumerate(
            ((len_hbm, len_ref), (wk_hbm, wk_buf.at[0]), (wq_hbm, wq_buf.at[0]))
        )
    ]
    k_load = [
        pltpu.make_async_copy(k_hbm.at[:, kv_cols(o)], xk.at[o], load_sem.at[4 + o])
        for o in range(n_head)
    ]
    v_load = pltpu.make_async_copy(v_hbm.at[:, kv_cols(0)], v_buf.at[own, :], load_sem.at[3])
    q_load = [
        pltpu.make_async_copy(q_hbm.at[:, q_cols(o)], xq.at[o], load_sem.at[4 + n_head + o])
        for o in range(n_head)
    ]
    for c in (*small, *k_load, v_load, *q_load):
        c.start()

    @pl.when(me != 0)
    def _():
        pl.semaphore_wait(barrier, 1)
        pl.semaphore_signal(here_sem, inc=1, device_id=(b, 0), device_id_type=MESH)

    @pl.when(me == 0)
    def _():
        pl.semaphore_wait(here_sem, n_head - 1)

    if n_head > 2:

        @pl.when(me == 0)
        def _():
            for o in others:
                pl.semaphore_signal(all_sem, inc=1, device_id=(b, o), device_id_type=MESH)

        @pl.when(me != 0)
        def _():
            pl.semaphore_wait(all_sem, 1)

    def remote(src, dst, send, recv, o):
        return pltpu.make_async_remote_copy(
            src_ref=src, dst_ref=dst, send_sem=send, recv_sem=recv,
            device_id=(b, peer(o)), device_id_type=MESH,
        )

    def w_copy(o, which):
        src, dst = ((wk_hbm, wk_buf), (wq_hbm, wq_buf))[which]
        slot = n_head - o
        return remote(
            src, dst.at[slot], w_send.at[slot - 1, which], w_recv.at[slot - 1, which], o
        )

    def v_copy(o):
        slot = n_head - o - 1
        return remote(
            v_hbm.at[:, kv_cols(o)], v_buf.at[own, :], kv_send.at[slot, 0], kv_recv.at[slot, 0], o
        )

    def k_copy(o):
        slot = n_head - o - 1
        return remote(
            uk_out.at[slot], uk_in.at[slot], kv_send.at[slot, 1], kv_recv.at[slot, 1], o
        )

    def q_copy(o, i):
        slot = n_head - o - 1
        return remote(
            uq_out.at[slot, i], uq_in.at[slot, i], q_send.at[slot, i], q_recv.at[slot, i], o
        )

    for o in others:
        w_copy(o, 0).start()
        w_copy(o, 1).start()
    for o in others:
        v_copy(o).start()

    @pl.when(me == 0)
    def _():
        def greet(i, _):
            @pl.when(i <= n_to)
            def _():
                pl.semaphore_signal(barrier, inc=1, device_id=(b + i, 0), device_id_type=MESH)

            @pl.when(i <= n_from)
            def _():
                pl.semaphore_signal(barrier, inc=1, device_id=(b - i, 0), device_id_type=MESH)

            return 0

        lax.fori_loop(1, reach + 1, greet, 0)

    for c in small:
        c.wait()
    docs = len_ref.shape[1]
    lens = jnp.broadcast_to(len_ref[...].astype(F32), (docs, docs))
    starts = jnp.sum(
        jnp.where(iota((docs, docs), 1) < iota((docs, docs), 0), lens, 0.0), 1, keepdims=True
    )

    def doc_start(pos):
        return jnp.max(jnp.where(starts <= pos, starts, -1.0), 0, keepdims=True)

    lane = iota((1, BLOCK), 1)
    for c in range(blocks):
        pos = (begin + c * BLOCK + lane).astype(F32)
        lo_ref[c] = jnp.broadcast_to(doc_start(pos), (8, BLOCK))
    v_ext[:, hd:, :] = jnp.ones((blocks, ZROWS, BLOCK), BF16)

    def pair_weights(o):
        zero = jnp.zeros((half, hd), BF16)
        return [
            jnp.concatenate(
                [
                    jnp.concatenate([wq_buf[o, h], zero], 1),
                    jnp.concatenate([zero, wq_buf[o, h + 1]], 1),
                ],
                0,
            )
            for h in range(0, heads, 2)
        ]

    def token_rows(i, n=1):
        return pl.ds(pl.multiple_of(i * BLOCK, BLOCK), n * BLOCK)

    def edge_at(pos):
        return doc_start(pos.astype(F32))

    def set_values(c):
        v_ext[c, :hd, :] = v_buf[token_rows(c), :].T

    def set_keys(c, phi):
        keys = phi.astype(BF16).T
        phi_k[c] = keys
        c0 = begin + c * BLOCK
        chosen = ((c0 + lane).astype(F32) >= edge_at(c0 + BLOCK - 1)).astype(F32).astype(BF16)
        fresh[c] = jnp.dot(v_ext[c] * chosen, keys, preferred_element_type=F32)

    k_load[0].wait()
    v_load.wait()

    def own_keys(i, _):
        p = lax.dot_general(
            wk_buf[0], xk[0, token_rows(i * step, step), :], NT, preferred_element_type=F32
        )
        phi = features(p)
        for j in range(step):
            set_values(me * per + i * step + j)
            set_keys(me * per + i * step + j, phi[:, j * BLOCK : (j + 1) * BLOCK])
        return 0

    lax.fori_loop(0, per // step, own_keys, 0, unroll=True)
    q_load[0].wait()
    weights = pair_weights(0)

    def own_queries(i, _):
        for n, w in enumerate(weights):
            x = xq[0, token_rows(i * step, step), 2 * n * hd : 2 * (n + 1) * hd]
            p = lax.dot_general(w, x, NT, preferred_element_type=F32)
            for m in range(2):
                phi = features(p[m * half : (m + 1) * half]).astype(BF16)
                h = 2 * n + m
                for j in range(step):
                    phi_q[me * per + i * step + j, :, h * hd : (h + 1) * hd] = phi[
                        :, j * BLOCK : (j + 1) * BLOCK
                    ]
        return 0

    lax.fori_loop(0, per // step, own_queries, 0, unroll=True)

    for o in others:
        w_copy(n_head - o, 0).wait_recv()
        k_load[o].wait()
        p = lax.dot_general(wk_buf[o], xk[o], NT, preferred_element_type=F32)
        uk_out[n_head - o - 1] = encode(p)
        k_copy(o).start()
    for o in others:
        w_copy(n_head - o, 1).wait_recv()
        q_load[o].wait()
        weights = pair_weights(o)
        for i in range(per // step):
            for n, w in enumerate(weights):
                x = xq[o, token_rows(i * step, step), 2 * n * hd : 2 * (n + 1) * hd]
                p = lax.dot_general(w, x, NT, preferred_element_type=F32)
                for m in range(2):
                    u = encode(p[m * half : (m + 1) * half])
                    h = 2 * n + m
                    for j in range(step):
                        uq_out[n_head - o - 1, i * step + j, h * half : (h + 1) * half, :] = u[
                            :, j * BLOCK : (j + 1) * BLOCK
                        ]
            for j in range(step):
                q_copy(o, i * step + j).start()

    within = [edge_at(begin + (c + 1) * BLOCK - 1) < (begin + c * BLOCK).astype(F32) for c in range(blocks)]
    across = [edge_at(begin + c * BLOCK - 1) < begin.astype(F32) for c in range(blocks)]
    before = edge_at(begin - 1)
    for o in others:
        v_copy(n_head - o).wait_recv()
        for i in range(per):
            set_values(peer(o) * per + i)
    for o in others:
        k_copy(n_head - o).wait_recv()
        phi = decode(uk_in[o - 1])
        for i in range(per):
            set_keys(peer(o) * per + i, phi[:, i * BLOCK : (i + 1) * BLOCK])

    total = jnp.zeros((hd + ZROWS, hd), F32)
    for c in range(blocks):
        carry[c] = total
        total = fresh[c] + jnp.where(within[c], total, 0.0)
    state_out[...] = total.astype(BF16)

    @pl.when(me == 0)
    def _():
        pl.semaphore_wait(barrier, n_to + n_from)
        for o in others:
            pl.semaphore_signal(ctx_sem, inc=1, device_id=(b, o), device_id_type=MESH)

    @pl.when(me != 0)
    def _():
        pl.semaphore_wait(ctx_sem, 1)

    def s_copy(i):
        return pltpu.make_async_remote_copy(
            src_ref=state_out,
            dst_ref=state_in.at[i - 1],
            send_sem=s_send.at[i - 1],
            recv_sem=s_recv.at[i - 1],
            device_id=(b + i, me),
            device_id_type=MESH,
        )

    def push(i, _):
        @pl.when(i <= n_to)
        def _():
            s_copy(i).start()

        return 0

    lax.fori_loop(1, reach + 1, push, 0)

    carry[blocks] = jnp.zeros((hd + ZROWS, hd), F32)

    def collect(i, _):
        @pl.when(i <= n_from)
        def _():
            s_copy(i).wait_recv()
            end = ((b - i + 1) * length - 1).astype(F32)
            carry[blocks] += jnp.where(end >= before, state_in[i - 1].astype(F32), 0.0)

        return 0

    lax.fori_loop(1, reach + 1, collect, 0)
    for c in range(blocks):
        held[c] = (carry[c] + jnp.where(across[c], carry[blocks], 0.0)).astype(BF16)

    def attend(c):
        c0 = begin + c * BLOCK
        q = phi_q[c]
        scores = jnp.dot(phi_k[c], q, preferred_element_type=F32)
        lo = lo_ref[c, 0:1, :]
        s_i = iota((BLOCK, BLOCK), 0)
        mask = (s_i <= iota((BLOCK, BLOCK), 1)) & ((c0 + s_i).astype(F32) >= lo)
        carried = (lo < c0.astype(F32)).astype(F32).astype(BF16)
        parts = [
            jnp.where(mask, scores[:, h * hd : (h + 1) * hd], 0.0).astype(BF16)
            for h in range(heads)
        ]
        old = q * jnp.concatenate([carried] * heads, 1)
        left = jnp.concatenate([v_ext[c], held[c]], 1)
        right = jnp.concatenate([jnp.concatenate(parts, 1), old], 0)
        acc = jnp.dot(left, right, preferred_element_type=F32)
        out = (acc[:hd] * (1.0 / acc[hd : hd + 1])).astype(BF16)
        for h in range(heads):
            out_ref[token_rows(c), h * hd : (h + 1) * hd] = out[:, h * hd : (h + 1) * hd].T

    def own_block(i, _):
        attend(me * per + i)
        return 0

    lax.fori_loop(0, per, own_block, 0, unroll=True)
    for o in others:
        first = peer(o) * per

        def peer_block(i, _):
            q_copy(n_head - o, i).wait_recv()
            for h in range(heads):
                phi_q[first + i, :, h * hd : (h + 1) * hd] = decode(
                    uq_in[o - 1, i, h * half : (h + 1) * half, :]
                ).astype(BF16)
            attend(first + i)
            return 0

        lax.fori_loop(0, per, peer_block, 0, unroll=True)

    for o in others:
        w_copy(o, 0).wait_send()
        w_copy(o, 1).wait_send()
        v_copy(o).wait_send()
        k_copy(o).wait_send()
        for i in range(per):
            q_copy(o, i).wait_send()

    def pushed(i, _):
        @pl.when(i <= n_to)
        def _():
            s_copy(i).wait_send()

        return 0

    lax.fori_loop(1, reach + 1, pushed, 0)


def body(n_ctx, n_head, queries, keys, values, q_feature, k_feature, doc_lengths):
    rows = queries.shape[0]
    heads, hd, half = q_feature.shape
    length = rows * n_head
    tokens = length * n_ctx
    blocks = length // BLOCK
    per = rows // BLOCK
    first = tokens // 2 - length // 2
    n0, n1 = first // length, (first + SECOND) // length
    reach = min(max(n0, n1 - n0, n_ctx - n1), n_ctx - 1)
    hbm = pl.BlockSpec(memory_space=pltpu.HBM)
    vmem = pl.BlockSpec(memory_space=pltpu.VMEM)
    dma, plain = pltpu.SemaphoreType.DMA, pltpu.SemaphoreType.REGULAR
    others = max(n_head - 1, 1)
    operands = (
        queries, keys, values,
        q_feature.transpose(0, 2, 1), k_feature[0].T,
        doc_lengths.reshape(1, -1),
    )
    return pl.pallas_call(
        functools.partial(kernel, n_ctx, n_head, n0, n1, reach),
        out_shape=jax.ShapeDtypeStruct((length, heads * hd), BF16),
        in_specs=[hbm] * 6,
        out_specs=vmem,
        scratch_shapes=[
            pltpu.VMEM((n_head, rows, heads * hd), BF16),
            pltpu.VMEM((n_head, rows, hd), BF16),
            pltpu.VMEM((length, hd), BF16),
            pltpu.VMEM((n_head, heads, half, hd), BF16),
            pltpu.VMEM((n_head, half, hd), BF16),
            pltpu.VMEM((1, doc_lengths.shape[0]), jnp.int32),
            pltpu.VMEM((others, half, rows), BF16),
            pltpu.VMEM((others, per, heads * half, BLOCK), BF16),
            pltpu.VMEM((others, half, rows), BF16),
            pltpu.VMEM((others, per, heads * half, BLOCK), BF16),
            pltpu.VMEM((blocks, BLOCK, 2 * half), BF16),
            pltpu.VMEM((blocks, hd + ZROWS, BLOCK), BF16),
            pltpu.VMEM((blocks, 2 * half, heads * BLOCK), BF16),
            pltpu.VMEM((blocks, hd + ZROWS, 2 * half), BF16),
            pltpu.VMEM((blocks + 1, hd + ZROWS, 2 * half), F32),
            pltpu.VMEM((blocks, hd + ZROWS, 2 * half), F32),
            pltpu.VMEM((blocks, 8, BLOCK), F32),
            pltpu.VMEM((hd + ZROWS, 2 * half), BF16),
            pltpu.VMEM((reach, hd + ZROWS, 2 * half), BF16),
            dma((4 + 2 * n_head,)),
            dma((others, 2)),
            dma((others, 2)),
            dma((others, 2)),
            dma((others, 2)),
            dma((others, per)),
            dma((others, per)),
            dma((reach,)),
            dma((reach,)),
            plain, plain, plain,
        ],
        compiler_params=pltpu.CompilerParams(
            collective_id=0, has_side_effects=True, vmem_limit_bytes=32 << 20
        ),
    )(*[pltpu.with_memory_space_constraint(a, pltpu.HBM) for a in operands])


def solution(mesh):
    placed = (
        P(("ctx", "head"), None),
        P(("ctx", "head"), None),
        P(("ctx", "head"), None),
        P("head", None, None),
        P("head", None, None),
        P(),
    )
    return jax.shard_map(
        functools.partial(body, mesh.shape["ctx"], mesh.shape["head"]),
        mesh=mesh,
        in_specs=placed,
        out_specs=P("ctx", "head"),
        check_vma=False,
    )
```

```python
import functools

import jax
import jax.numpy as jnp
from jax import lax
from jax.experimental import pallas as pl
from jax.experimental.pallas import tpu as pltpu
from jax.sharding import PartitionSpec as P

MESH = pl.DeviceIdType.MESH
F32 = jnp.float32
BF16 = jnp.bfloat16
NT = (((1,), (1,)), ((), ()))
SECOND = 3 * 1024
ZROWS = 16
BLOCK = 128
SPAN = 80.0


def iota(shape, dim):
    return lax.broadcasted_iota(jnp.int32, shape, dim)


def extremes(p):
    return jnp.max(p, 0, keepdims=True), jnp.min(p, 0, keepdims=True)


def features(p):
    top, low = extremes(p)
    up, down = jnp.exp(p - top), jnp.exp(low - p)
    up = up * (1.0 / jnp.sum(up, 0, keepdims=True))
    down = down * (1.0 / jnp.sum(down, 0, keepdims=True))
    return jnp.concatenate([up, down], 0)


def encode(p):
    top, low = extremes(p)
    reach = jnp.minimum(SPAN, 0.5 * (top - low))
    return jnp.exp(jnp.maximum(p - top + reach, 0.0) + jnp.minimum(p - low - reach, 0.0)).astype(BF16)


def decode(u):
    up = u.astype(F32)
    down = 1.0 / up
    up = up * (1.0 / jnp.sum(up, 0, keepdims=True))
    down = down * (1.0 / jnp.sum(down, 0, keepdims=True))
    return jnp.concatenate([up, down], 0)


def kernel(
    n_ctx, n_head, n0, n1, reach,
    q_hbm, k_hbm, v_hbm, wq_hbm, wk_hbm, len_hbm, out_ref,
    xq, xk, v_buf, wq_buf, wk_buf, len_ref,
    uk_out, uq_out, uk_in, uq_in, phi_k, v_ext, phi_q, mixed, carry, fresh, lo_ref, state_out, state_in,
    load_sem, w_send, w_recv, kv_send, kv_recv, q_send, q_recv, s_send, s_recv,
    here_sem, all_sem, ctx_sem,
):
    me, b = lax.axis_index("head"), lax.axis_index("ctx")
    rows, hd = q_hbm.shape[0], BLOCK
    heads = wq_hbm.shape[0]
    half = hd // 2
    wide = heads * hd
    blocks = phi_k.shape[0]
    per = rows // BLOCK
    step = min(2, per)
    length = blocks * BLOCK
    begin = b * length
    others = range(1, n_head)

    def peer(o):
        return lax.rem(me + o, n_head)

    def last_of(j):
        return jnp.where(j < n0, n0 - 1, jnp.where(j < n1, n1 - 1, n_ctx - 1))

    def first_of(j):
        return jnp.where(j < n0, 0, jnp.where(j < n1, n0, n1))

    n_to = jnp.minimum(last_of(b) + 1, n_ctx - 1) - b
    n_from = jnp.where(b == 0, 0, b - first_of(b - 1))

    barrier = pltpu.get_barrier_semaphore()

    @pl.when(me == 0)
    def _():
        for o in others:
            pl.semaphore_signal(barrier, inc=1, device_id=(b, o), device_id_type=MESH)

    own = pl.ds(pl.multiple_of(me * rows, rows), rows)

    def q_cols(o):
        return pl.ds(pl.multiple_of(peer(o) * wide, wide), wide)

    def kv_cols(o):
        return pl.ds(pl.multiple_of(peer(o) * hd, hd), hd)

    small = [
        pltpu.make_async_copy(src, dst, load_sem.at[i])
        for i, (src, dst) in enumerate(
            ((len_hbm, len_ref), (wk_hbm, wk_buf.at[0]), (wq_hbm, wq_buf.at[0]))
        )
    ]
    k_load = [
        pltpu.make_async_copy(k_hbm.at[:, kv_cols(o)], xk.at[o], load_sem.at[4 + o])
        for o in range(n_head)
    ]
    v_load = pltpu.make_async_copy(v_hbm.at[:, kv_cols(0)], v_buf.at[own, :], load_sem.at[3])
    q_load = [
        pltpu.make_async_copy(q_hbm.at[:, q_cols(o)], xq.at[o], load_sem.at[4 + n_head + o])
        for o in range(n_head)
    ]
    for c in (*small, *k_load, v_load, *q_load):
        c.start()

    @pl.when(me != 0)
    def _():
        pl.semaphore_wait(barrier, 1)
        pl.semaphore_signal(here_sem, inc=1, device_id=(b, 0), device_id_type=MESH)

    @pl.when(me == 0)
    def _():
        pl.semaphore_wait(here_sem, n_head - 1)

    if n_head > 2:

        @pl.when(me == 0)
        def _():
            for o in others:
                pl.semaphore_signal(all_sem, inc=1, device_id=(b, o), device_id_type=MESH)

        @pl.when(me != 0)
        def _():
            pl.semaphore_wait(all_sem, 1)

    def remote(src, dst, send, recv, o):
        return pltpu.make_async_remote_copy(
            src_ref=src, dst_ref=dst, send_sem=send, recv_sem=recv,
            device_id=(b, peer(o)), device_id_type=MESH,
        )

    def w_copy(o, which):
        src, dst = ((wk_hbm, wk_buf), (wq_hbm, wq_buf))[which]
        slot = n_head - o
        return remote(
            src, dst.at[slot], w_send.at[slot - 1, which], w_recv.at[slot - 1, which], o
        )

    def v_copy(o):
        slot = n_head - o - 1
        return remote(
            v_hbm.at[:, kv_cols(o)], v_buf.at[own, :], kv_send.at[slot, 0], kv_recv.at[slot, 0], o
        )

    def k_copy(o):
        slot = n_head - o - 1
        return remote(
            uk_out.at[slot], uk_in.at[slot], kv_send.at[slot, 1], kv_recv.at[slot, 1], o
        )

    def q_copy(o, i):
        slot = n_head - o - 1
        return remote(
            uq_out.at[slot, i], uq_in.at[slot, i], q_send.at[slot, i], q_recv.at[slot, i], o
        )

    for o in others:
        w_copy(o, 0).start()
        w_copy(o, 1).start()
    for o in others:
        v_copy(o).start()

    @pl.when(me == 0)
    def _():
        def greet(i, _):
            @pl.when(i <= n_to)
            def _():
                pl.semaphore_signal(barrier, inc=1, device_id=(b + i, 0), device_id_type=MESH)

            @pl.when(i <= n_from)
            def _():
                pl.semaphore_signal(barrier, inc=1, device_id=(b - i, 0), device_id_type=MESH)

            return 0

        lax.fori_loop(1, reach + 1, greet, 0)

    for c in small:
        c.wait()
    docs = len_ref.shape[1]
    lens = jnp.broadcast_to(len_ref[...].astype(F32), (docs, docs))
    starts = jnp.sum(
        jnp.where(iota((docs, docs), 1) < iota((docs, docs), 0), lens, 0.0), 1, keepdims=True
    )

    def doc_start(pos):
        return jnp.max(jnp.where(starts <= pos, starts, -1.0), 0, keepdims=True)

    lane = iota((1, BLOCK), 1)
    for c in range(blocks):
        pos = (begin + c * BLOCK + lane).astype(F32)
        lo_ref[c] = jnp.broadcast_to(doc_start(pos), (8, BLOCK))
    v_ext[:, hd:, :] = jnp.ones((blocks, ZROWS, BLOCK), BF16)

    def pair_weights(o):
        zero = jnp.zeros((half, hd), BF16)
        return [
            jnp.concatenate(
                [
                    jnp.concatenate([wq_buf[o, h], zero], 1),
                    jnp.concatenate([zero, wq_buf[o, h + 1]], 1),
                ],
                0,
            )
            for h in range(0, heads, 2)
        ]

    def token_rows(i, n=1):
        return pl.ds(pl.multiple_of(i * BLOCK, BLOCK), n * BLOCK)

    def edge_at(pos):
        return doc_start(pos.astype(F32))

    def set_values(c):
        v_ext[c, :hd, :] = v_buf[token_rows(c), :].T

    def set_keys(c, phi):
        keys = phi.astype(BF16).T
        phi_k[c] = keys
        c0 = begin + c * BLOCK
        chosen = ((c0 + lane).astype(F32) >= edge_at(c0 + BLOCK - 1)).astype(F32).astype(BF16)
        fresh[c] = jnp.dot(v_ext[c] * chosen, keys, preferred_element_type=F32)

    k_load[0].wait()
    v_load.wait()

    def own_keys(i, _):
        p = lax.dot_general(
            wk_buf[0], xk[0, token_rows(i * step, step), :], NT, preferred_element_type=F32
        )
        phi = features(p)
        for j in range(step):
            set_values(me * per + i * step + j)
            set_keys(me * per + i * step + j, phi[:, j * BLOCK : (j + 1) * BLOCK])
        return 0

    lax.fori_loop(0, per // step, own_keys, 0, unroll=True)
    q_load[0].wait()
    weights = pair_weights(0)

    def own_queries(i, _):
        for n, w in enumerate(weights):
            x = xq[0, token_rows(i * step, step), 2 * n * hd : 2 * (n + 1) * hd]
            p = lax.dot_general(w, x, NT, preferred_element_type=F32)
            for m in range(2):
                phi = features(p[m * half : (m + 1) * half]).astype(BF16)
                h = 2 * n + m
                for j in range(step):
                    phi_q[i * step + j, :, h * hd : (h + 1) * hd] = phi[
                        :, j * BLOCK : (j + 1) * BLOCK
                    ]
        return 0

    lax.fori_loop(0, per // step, own_queries, 0, unroll=True)

    for o in others:
        w_copy(n_head - o, 0).wait_recv()
        k_load[o].wait()
        p = lax.dot_general(wk_buf[o], xk[o], NT, preferred_element_type=F32)
        uk_out[n_head - o - 1] = encode(p)
        k_copy(o).start()
    for o in others:
        w_copy(n_head - o, 1).wait_recv()
        q_load[o].wait()
        weights = pair_weights(o)
        for i in range(per // step):
            for n, w in enumerate(weights):
                x = xq[o, token_rows(i * step, step), 2 * n * hd : 2 * (n + 1) * hd]
                p = lax.dot_general(w, x, NT, preferred_element_type=F32)
                for m in range(2):
                    u = encode(p[m * half : (m + 1) * half])
                    h = 2 * n + m
                    for j in range(step):
                        uq_out[n_head - o - 1, i * step + j, h * half : (h + 1) * half, :] = u[
                            :, j * BLOCK : (j + 1) * BLOCK
                        ]
            for j in range(step):
                q_copy(o, i * step + j).start()

    within = [edge_at(begin + (c + 1) * BLOCK - 1) < (begin + c * BLOCK).astype(F32) for c in range(blocks)]
    across = [edge_at(begin + c * BLOCK - 1) < begin.astype(F32) for c in range(blocks)]
    before = edge_at(begin - 1)
    for o in others:
        v_copy(n_head - o).wait_recv()
        for i in range(per):
            set_values(peer(o) * per + i)
    for o in others:
        k_copy(n_head - o).wait_recv()
        phi = decode(uk_in[o - 1])
        for i in range(per):
            set_keys(peer(o) * per + i, phi[:, i * BLOCK : (i + 1) * BLOCK])

    total = jnp.zeros((hd + ZROWS, hd), F32)
    for c in range(blocks):
        carry[c] = total
        total = fresh[c] + jnp.where(within[c], total, 0.0)
    state_out[...] = total.astype(BF16)

    @pl.when(me == 0)
    def _():
        pl.semaphore_wait(barrier, n_to + n_from)
        for o in others:
            pl.semaphore_signal(ctx_sem, inc=1, device_id=(b, o), device_id_type=MESH)

    @pl.when(me != 0)
    def _():
        pl.semaphore_wait(ctx_sem, 1)

    def s_copy(i):
        return pltpu.make_async_remote_copy(
            src_ref=state_out,
            dst_ref=state_in.at[i - 1],
            send_sem=s_send.at[i - 1],
            recv_sem=s_recv.at[i - 1],
            device_id=(b + i, me),
            device_id_type=MESH,
        )

    def push(i, _):
        @pl.when(i <= n_to)
        def _():
            s_copy(i).start()

        return 0

    lax.fori_loop(1, reach + 1, push, 0)

    def weigh(c, q):
        c0 = begin + c * BLOCK
        scores = jnp.dot(phi_k[c], q, preferred_element_type=F32)
        lo = lo_ref[c, 0:1, :]
        s_i = iota((BLOCK, BLOCK), 0)
        mask = (s_i <= iota((BLOCK, BLOCK), 1)) & ((c0 + s_i).astype(F32) >= lo)
        carried = (lo < c0.astype(F32)).astype(F32).astype(BF16)
        for h in range(heads):
            cols = slice(h * hd, (h + 1) * hd)
            mixed[c, :BLOCK, cols] = jnp.where(mask, scores[:, cols], 0.0).astype(BF16)
        mixed[c, BLOCK:, :] = q * jnp.concatenate([carried] * heads, 1)

    def finish(c):
        left = jnp.concatenate([v_ext[c], carry[c].astype(BF16)], 1)
        acc = jnp.dot(left, mixed[c], preferred_element_type=F32)
        out = (acc[:hd] * (1.0 / acc[hd : hd + 1])).astype(BF16)
        for h in range(heads):
            out_ref[token_rows(c), h * hd : (h + 1) * hd] = out[:, h * hd : (h + 1) * hd].T

    def arrived(o, i):
        q_copy(n_head - o, i).wait_recv()
        u = uq_in[o - 1, i]
        return jnp.concatenate(
            [decode(u[h * half : (h + 1) * half]).astype(BF16) for h in range(heads)], 1
        )

    for i in range(per):
        weigh(me * per + i, phi_q[i])
    order = [(o, i) for o in others for i in range(per)]
    for o, i in order[:-1]:
        weigh(peer(o) * per + i, arrived(o, i))

    carry[blocks] = jnp.zeros((hd + ZROWS, hd), F32)

    def collect(i, _):
        @pl.when(i <= n_from)
        def _():
            s_copy(i).wait_recv()
            end = ((b - i + 1) * length - 1).astype(F32)
            carry[blocks] += jnp.where(end >= before, state_in[i - 1].astype(F32), 0.0)

        return 0

    lax.fori_loop(1, reach + 1, collect, 0)
    for c in range(blocks):
        carry[c] += jnp.where(across[c], carry[blocks], 0.0)

    for i in range(per):
        finish(me * per + i)
    for o, i in order[:-1]:
        finish(peer(o) * per + i)
    for o, i in order[-1:]:
        weigh(peer(o) * per + i, arrived(o, i))
        finish(peer(o) * per + i)

    for o in others:
        w_copy(o, 0).wait_send()
        w_copy(o, 1).wait_send()
        v_copy(o).wait_send()
        k_copy(o).wait_send()
        for i in range(per):
            q_copy(o, i).wait_send()

    def pushed(i, _):
        @pl.when(i <= n_to)
        def _():
            s_copy(i).wait_send()

        return 0

    lax.fori_loop(1, reach + 1, pushed, 0)


def body(n_ctx, n_head, queries, keys, values, q_feature, k_feature, doc_lengths):
    rows = queries.shape[0]
    heads, hd, half = q_feature.shape
    length = rows * n_head
    tokens = length * n_ctx
    blocks = length // BLOCK
    per = rows // BLOCK
    first = tokens // 2 - length // 2
    n0, n1 = first // length, (first + SECOND) // length
    reach = min(max(n0, n1 - n0, n_ctx - n1), n_ctx - 1)
    hbm = pl.BlockSpec(memory_space=pltpu.HBM)
    vmem = pl.BlockSpec(memory_space=pltpu.VMEM)
    dma, plain = pltpu.SemaphoreType.DMA, pltpu.SemaphoreType.REGULAR
    others = max(n_head - 1, 1)
    operands = (
        queries, keys, values,
        q_feature.transpose(0, 2, 1), k_feature[0].T,
        doc_lengths.reshape(1, -1),
    )
    return pl.pallas_call(
        functools.partial(kernel, n_ctx, n_head, n0, n1, reach),
        out_shape=jax.ShapeDtypeStruct((length, heads * hd), BF16),
        in_specs=[hbm] * 6,
        out_specs=vmem,
        scratch_shapes=[
            pltpu.VMEM((n_head, rows, heads * hd), BF16),
            pltpu.VMEM((n_head, rows, hd), BF16),
            pltpu.VMEM((length, hd), BF16),
            pltpu.VMEM((n_head, heads, half, hd), BF16),
            pltpu.VMEM((n_head, half, hd), BF16),
            pltpu.VMEM((1, doc_lengths.shape[0]), jnp.int32),
            pltpu.VMEM((others, half, rows), BF16),
            pltpu.VMEM((others, per, heads * half, BLOCK), BF16),
            pltpu.VMEM((others, half, rows), BF16),
            pltpu.VMEM((others, per, heads * half, BLOCK), BF16),
            pltpu.VMEM((blocks, BLOCK, 2 * half), BF16),
            pltpu.VMEM((blocks, hd + ZROWS, BLOCK), BF16),
            pltpu.VMEM((per, 2 * half, heads * BLOCK), BF16),
            pltpu.VMEM((blocks, BLOCK + 2 * half, heads * BLOCK), BF16),
            pltpu.VMEM((blocks + 1, hd + ZROWS, 2 * half), F32),
            pltpu.VMEM((blocks, hd + ZROWS, 2 * half), F32),
            pltpu.VMEM((blocks, 8, BLOCK), F32),
            pltpu.VMEM((hd + ZROWS, 2 * half), BF16),
            pltpu.VMEM((reach, hd + ZROWS, 2 * half), BF16),
            dma((4 + 2 * n_head,)),
            dma((others, 2)),
            dma((others, 2)),
            dma((others, 2)),
            dma((others, 2)),
            dma((others, per)),
            dma((others, per)),
            dma((reach,)),
            dma((reach,)),
            plain, plain, plain,
        ],
        compiler_params=pltpu.CompilerParams(
            collective_id=0, has_side_effects=True, vmem_limit_bytes=32 << 20
        ),
    )(*[pltpu.with_memory_space_constraint(a, pltpu.HBM) for a in operands])


def solution(mesh):
    placed = (
        P(("ctx", "head"), None),
        P(("ctx", "head"), None),
        P(("ctx", "head"), None),
        P("head", None, None),
        P("head", None, None),
        P(),
    )
    return jax.shard_map(
        functools.partial(body, mesh.shape["ctx"], mesh.shape["head"]),
        mesh=mesh,
        in_specs=placed,
        out_specs=P("ctx", "head"),
        check_vma=False,
    )
```

```python
import functools

import jax
import jax.numpy as jnp
from jax import lax
from jax.experimental import pallas as pl
from jax.experimental.pallas import tpu as pltpu
from jax.sharding import PartitionSpec as P

MESH = pl.DeviceIdType.MESH
F32 = jnp.float32
BF16 = jnp.bfloat16
NT = (((1,), (1,)), ((), ()))
SECOND = 3 * 1024
ZROWS = 16
BLOCK = 128
SPAN = 80.0
EARLY = 1


def iota(shape, dim):
    return lax.broadcasted_iota(jnp.int32, shape, dim)


def extremes(p):
    return jnp.max(p, 0, keepdims=True), jnp.min(p, 0, keepdims=True)


def features(p):
    top, low = extremes(p)
    up, down = jnp.exp(p - top), jnp.exp(low - p)
    up = up * (1.0 / jnp.sum(up, 0, keepdims=True))
    down = down * (1.0 / jnp.sum(down, 0, keepdims=True))
    return jnp.concatenate([up, down], 0)


def encode(p):
    top, low = extremes(p)
    reach = jnp.minimum(SPAN, 0.5 * (top - low))
    return jnp.exp(jnp.maximum(p - top + reach, 0.0) + jnp.minimum(p - low - reach, 0.0)).astype(BF16)


def decode(u):
    up = u.astype(F32)
    down = 1.0 / up
    up = up * (1.0 / jnp.sum(up, 0, keepdims=True))
    down = down * (1.0 / jnp.sum(down, 0, keepdims=True))
    return jnp.concatenate([up, down], 0)


def span(n_ctx, n0, n1, b):
    def last_of(j):
        return jnp.where(j < n0, n0 - 1, jnp.where(j < n1, n1 - 1, n_ctx - 1))

    def first_of(j):
        return jnp.where(j < n0, 0, jnp.where(j < n1, n0, n1))

    return jnp.minimum(last_of(b) + 1, n_ctx - 1) - b, jnp.where(b == 0, 0, b - first_of(b - 1))


def token_rows(i, n=1):
    if isinstance(i, int):
        return pl.ds(i * BLOCK, n * BLOCK)
    return pl.ds(pl.multiple_of(i * BLOCK, BLOCK), n * BLOCK)


def finish(c, v_ext, held, mixed, out):
    hd = BLOCK
    left = jnp.concatenate([v_ext[c], held[c]], 1)
    acc = jnp.dot(left, mixed[c], preferred_element_type=F32)
    done = (acc[:hd] * (1.0 / acc[hd : hd + 1])).astype(BF16)
    for h in range(mixed.shape[2] // hd):
        out[token_rows(c), h * hd : (h + 1) * hd] = done[:, h * hd : (h + 1) * hd].T


def kernel(
    n_ctx, n_head, n0, n1, reach,
    q_hbm, k_hbm, v_hbm, wq_hbm, wk_hbm, len_hbm, v_ext, held, mixed, out,
    xq, xk, v_buf, wq_buf, wk_buf, len_ref,
    uk_out, uq_out, uk_in, uq_in, phi_k, phi_q, carry, fresh, lo_ref, state_out, state_in,
    load_sem, w_send, w_recv, kv_send, kv_recv, q_send, q_recv, s_send, s_recv,
    here_sem, all_sem, ctx_sem, turn_sem,
):
    me, b = lax.axis_index("head"), lax.axis_index("ctx")
    rows, hd = q_hbm.shape[0], BLOCK
    heads = wq_hbm.shape[0]
    half = hd // 2
    wide = heads * hd
    blocks = phi_k.shape[0]
    per = rows // BLOCK
    step = min(2, per)
    hold = per - 1 if per >= 4 and n_ctx % 2 == 0 else per
    length = blocks * BLOCK
    begin = b * length
    others = range(1, n_head)
    second = lax.rem(b, 2)

    def peer(o):
        return lax.rem(me + o, n_head)

    n_to, n_from = span(n_ctx, n0, n1, b)
    early = n_from <= EARLY

    barrier = pltpu.get_barrier_semaphore()

    @pl.when(me == 0)
    def _():
        for o in others:
            pl.semaphore_signal(barrier, inc=1, device_id=(b, o), device_id_type=MESH)

    own = pl.ds(pl.multiple_of(me * rows, rows), rows)

    def q_cols(o):
        return pl.ds(pl.multiple_of(peer(o) * wide, wide), wide)

    def kv_cols(o):
        return pl.ds(pl.multiple_of(peer(o) * hd, hd), hd)

    small = [
        pltpu.make_async_copy(src, dst, load_sem.at[i])
        for i, (src, dst) in enumerate(
            ((len_hbm, len_ref), (wk_hbm, wk_buf.at[0]), (wq_hbm, wq_buf.at[0]))
        )
    ]
    k_load = [
        pltpu.make_async_copy(k_hbm.at[:, kv_cols(o)], xk.at[o], load_sem.at[4 + o])
        for o in range(n_head)
    ]
    v_load = pltpu.make_async_copy(v_hbm.at[:, kv_cols(0)], v_buf.at[own, :], load_sem.at[3])
    q_load = [
        pltpu.make_async_copy(q_hbm.at[:, q_cols(o)], xq.at[o], load_sem.at[4 + n_head + o])
        for o in range(n_head)
    ]
    for c in (*small, *k_load, v_load, *q_load):
        c.start()

    @pl.when(me != 0)
    def _():
        pl.semaphore_wait(barrier, 1)
        pl.semaphore_signal(here_sem, inc=1, device_id=(b, 0), device_id_type=MESH)

    @pl.when(me == 0)
    def _():
        pl.semaphore_wait(here_sem, n_head - 1)

    if n_head > 2:

        @pl.when(me == 0)
        def _():
            for o in others:
                pl.semaphore_signal(all_sem, inc=1, device_id=(b, o), device_id_type=MESH)

        @pl.when(me != 0)
        def _():
            pl.semaphore_wait(all_sem, 1)

    def remote(src, dst, send, recv, o):
        return pltpu.make_async_remote_copy(
            src_ref=src, dst_ref=dst, send_sem=send, recv_sem=recv,
            device_id=(b, peer(o)), device_id_type=MESH,
        )

    def w_copy(o, which):
        src, dst = ((wk_hbm, wk_buf), (wq_hbm, wq_buf))[which]
        slot = n_head - o
        return remote(
            src, dst.at[slot], w_send.at[slot - 1, which], w_recv.at[slot - 1, which], o
        )

    def v_copy(o):
        slot = n_head - o - 1
        return remote(
            v_hbm.at[:, kv_cols(o)], v_buf.at[own, :], kv_send.at[slot, 0], kv_recv.at[slot, 0], o
        )

    def k_copy(o):
        slot = n_head - o - 1
        return remote(
            uk_out.at[slot], uk_in.at[slot], kv_send.at[slot, 1], kv_recv.at[slot, 1], o
        )

    def q_copy(o, i):
        slot = n_head - o - 1
        return remote(
            uq_out.at[slot, i], uq_in.at[slot, i], q_send.at[slot, i], q_recv.at[slot, i], o
        )

    for o in others:
        w_copy(o, 0).start()
        w_copy(o, 1).start()
    for o in others:
        v_copy(o).start()

    @pl.when(me == 0)
    def _():
        def greet(i, _):
            @pl.when(i <= n_to)
            def _():
                pl.semaphore_signal(barrier, inc=1, device_id=(b + i, 0), device_id_type=MESH)

            @pl.when(i <= n_from)
            def _():
                pl.semaphore_signal(barrier, inc=1, device_id=(b - i, 0), device_id_type=MESH)

            return 0

        lax.fori_loop(1, reach + 1, greet, 0)

    for c in small:
        c.wait()
    docs = len_ref.shape[1]
    lens = jnp.broadcast_to(len_ref[...].astype(F32), (docs, docs))
    starts = jnp.sum(
        jnp.where(iota((docs, docs), 1) < iota((docs, docs), 0), lens, 0.0), 1, keepdims=True
    )

    def doc_start(pos):
        return jnp.max(jnp.where(starts <= pos, starts, -1.0), 0, keepdims=True)

    lane = iota((1, BLOCK), 1)
    for c in range(blocks):
        pos = (begin + c * BLOCK + lane).astype(F32)
        lo_ref[c] = jnp.broadcast_to(doc_start(pos), (8, BLOCK))
    v_ext[:, hd:, :] = jnp.ones((blocks, ZROWS, BLOCK), BF16)

    def pair_weights(o):
        zero = jnp.zeros((half, hd), BF16)
        return [
            jnp.concatenate(
                [
                    jnp.concatenate([wq_buf[o, h], zero], 1),
                    jnp.concatenate([zero, wq_buf[o, h + 1]], 1),
                ],
                0,
            )
            for h in range(0, heads, 2)
        ]

    def edge_at(pos):
        return doc_start(pos.astype(F32))

    def set_values(c):
        v_ext[c, :hd, :] = v_buf[token_rows(c), :].T

    def set_keys(c, phi):
        keys = phi.astype(BF16).T
        phi_k[c] = keys
        c0 = begin + c * BLOCK
        chosen = ((c0 + lane).astype(F32) >= edge_at(c0 + BLOCK - 1)).astype(F32).astype(BF16)
        fresh[c] = jnp.dot(v_ext[c] * chosen, keys, preferred_element_type=F32)

    k_load[0].wait()
    v_load.wait()

    def own_keys(i, _):
        p = lax.dot_general(
            wk_buf[0], xk[0, token_rows(i * step, step), :], NT, preferred_element_type=F32
        )
        phi = features(p)
        for j in range(step):
            set_values(me * per + i * step + j)
            set_keys(me * per + i * step + j, phi[:, j * BLOCK : (j + 1) * BLOCK])
        return 0

    lax.fori_loop(0, per // step, own_keys, 0, unroll=True)
    q_load[0].wait()
    weights = pair_weights(0)

    def own_queries(i, _):
        for n, w in enumerate(weights):
            x = xq[0, token_rows(i * step, step), 2 * n * hd : 2 * (n + 1) * hd]
            p = lax.dot_general(w, x, NT, preferred_element_type=F32)
            for m in range(2):
                phi = features(p[m * half : (m + 1) * half]).astype(BF16)
                h = 2 * n + m
                for j in range(step):
                    phi_q[i * step + j, :, h * hd : (h + 1) * hd] = phi[
                        :, j * BLOCK : (j + 1) * BLOCK
                    ]
        return 0

    lax.fori_loop(0, per // step, own_queries, 0, unroll=True)

    for o in others:
        w_copy(n_head - o, 0).wait_recv()
        k_load[o].wait()
        p = lax.dot_general(wk_buf[o], xk[o], NT, preferred_element_type=F32)
        uk_out[n_head - o - 1] = encode(p)
        k_copy(o).start()
    for o in others:
        w_copy(n_head - o, 1).wait_recv()
        q_load[o].wait()
        weights = pair_weights(o)
        for i in range(per // step):
            for n, w in enumerate(weights):
                x = xq[o, token_rows(i * step, step), 2 * n * hd : 2 * (n + 1) * hd]
                p = lax.dot_general(w, x, NT, preferred_element_type=F32)
                for m in range(2):
                    u = encode(p[m * half : (m + 1) * half])
                    h = 2 * n + m
                    for j in range(step):
                        uq_out[n_head - o - 1, i * step + j, h * half : (h + 1) * half, :] = u[
                            :, j * BLOCK : (j + 1) * BLOCK
                        ]
            for j in range(step):
                if i * step + j < hold:
                    q_copy(o, i * step + j).start()
                else:

                    @pl.when(second == 0)
                    def _(copy=q_copy(o, i * step + j)):
                        copy.start()

    within = [edge_at(begin + (c + 1) * BLOCK - 1) < (begin + c * BLOCK).astype(F32) for c in range(blocks)]
    across = [edge_at(begin + c * BLOCK - 1) < begin.astype(F32) for c in range(blocks)]
    before = edge_at(begin - 1)
    for o in others:
        v_copy(n_head - o).wait_recv()
        for i in range(per):
            set_values(peer(o) * per + i)
    for o in others:
        k_copy(n_head - o).wait_recv()
        phi = decode(uk_in[o - 1])
        for i in range(per):
            set_keys(peer(o) * per + i, phi[:, i * BLOCK : (i + 1) * BLOCK])

    total = jnp.zeros((hd + ZROWS, hd), F32)
    for c in range(blocks):
        carry[c] = total
        total = fresh[c] + jnp.where(within[c], total, 0.0)
    state_out[...] = total.astype(BF16)

    @pl.when(me == 0)
    def _():
        pl.semaphore_wait(barrier, n_to + n_from)
        for o in others:
            pl.semaphore_signal(ctx_sem, inc=1, device_id=(b, o), device_id_type=MESH)

    @pl.when(me != 0)
    def _():
        pl.semaphore_wait(ctx_sem, 1)

    def s_copy(i):
        return pltpu.make_async_remote_copy(
            src_ref=state_out,
            dst_ref=state_in.at[i - 1],
            send_sem=s_send.at[i - 1],
            recv_sem=s_recv.at[i - 1],
            device_id=(b + i, me),
            device_id_type=MESH,
        )

    def push(i, _):
        @pl.when(i <= n_to)
        def _():
            s_copy(i).start()

        return 0

    lax.fori_loop(1, reach + 1, push, 0)

    if hold < per:

        @pl.when(second == 0)
        def _():
            for o in others:
                q_copy(o, per - 3).wait_send()
            pl.semaphore_signal(turn_sem, inc=1, device_id=(b + 1, me), device_id_type=MESH)

        @pl.when(second == 1)
        def _():
            pl.semaphore_wait(turn_sem, 1)
            for o in others:
                for i in range(hold, per):
                    q_copy(o, i).start()


    def weigh(c, q):
        c0 = begin + c * BLOCK
        scores = jnp.dot(phi_k[c], q, preferred_element_type=F32)
        lo = lo_ref[c, 0:1, :]
        s_i = iota((BLOCK, BLOCK), 0)
        mask = (s_i <= iota((BLOCK, BLOCK), 1)) & ((c0 + s_i).astype(F32) >= lo)
        carried = (lo < c0.astype(F32)).astype(F32).astype(BF16)
        for h in range(heads):
            cols = slice(h * hd, (h + 1) * hd)
            mixed[c, :BLOCK, cols] = jnp.where(mask, scores[:, cols], 0.0).astype(BF16)
        mixed[c, BLOCK:, :] = q * jnp.concatenate([carried] * heads, 1)

    def arrived(o, i):
        q_copy(n_head - o, i).wait_recv()
        u = uq_in[o - 1, i]
        return jnp.concatenate(
            [decode(u[h * half : (h + 1) * half]).astype(BF16) for h in range(heads)], 1
        )

    def collect(i, _):
        @pl.when(i <= n_from)
        def _():
            s_copy(i).wait_recv()
            end = ((b - i + 1) * length - 1).astype(F32)
            carry[blocks] += jnp.where(end >= before, state_in[i - 1].astype(F32), 0.0)

        return 0

    def enter():
        carry[blocks] = jnp.zeros((hd + ZROWS, hd), F32)
        lax.fori_loop(1, reach + 1, collect, 0)
        for c in range(blocks):
            held[c] = (carry[c] + jnp.where(across[c], carry[blocks], 0.0)).astype(BF16)

    order = [(o, i) for o in others for i in range(per)]
    for i in range(per):
        weigh(me * per + i, phi_q[i])
    for o, i in order[:-1]:
        weigh(peer(o) * per + i, arrived(o, i))

    @pl.when(early)
    def _():
        enter()
        for o, i in [(0, i) for i in range(per)] + order[:-1]:
            finish(peer(o) * per + i, v_ext, held, mixed, out)

    for o, i in order[-1:]:
        weigh(peer(o) * per + i, arrived(o, i))

    @pl.when(jnp.logical_not(early))
    def _():
        enter()

    for o in others:
        w_copy(o, 0).wait_send()
        w_copy(o, 1).wait_send()
        v_copy(o).wait_send()
        k_copy(o).wait_send()
        for i in range(per):
            if hold < per and i == per - 3:

                @pl.when(second == 1)
                def _(copy=q_copy(o, i)):
                    copy.wait_send()

            else:
                q_copy(o, i).wait_send()

    def pushed(i, _):
        @pl.when(i <= n_to)
        def _():
            s_copy(i).wait_send()

        return 0

    lax.fori_loop(1, reach + 1, pushed, 0)


def last_kernel(n_ctx, n_head, n0, n1, v_ext, held, mixed, made, out_hbm, out, out_sem):
    me, b = lax.axis_index("head"), lax.axis_index("ctx")
    blocks = mixed.shape[0]
    per = blocks // n_head
    early = span(n_ctx, n0, n1, b)[1] <= EARLY
    last = lax.rem(me + n_head - 1, n_head) * per + per - 1

    def write(c, src):
        rows = token_rows(c)
        return pltpu.make_async_copy(src.at[rows], out_hbm.at[rows], out_sem.at[c])

    @pl.when(early)
    def _():
        for c in range(blocks):

            @pl.when(c != last)
            def _(c=c):
                write(c, made).start()

        finish(last, v_ext, held, mixed, out)
        write(last, out).start()

    @pl.when(jnp.logical_not(early))
    def _():
        for c in range(blocks):
            finish(c, v_ext, held, mixed, out)
            write(c, out).start()

    for c in range(blocks):
        write(c, out).wait()


def body(n_ctx, n_head, queries, keys, values, q_feature, k_feature, doc_lengths):
    rows = queries.shape[0]
    heads, hd, half = q_feature.shape
    length = rows * n_head
    tokens = length * n_ctx
    blocks = length // BLOCK
    per = rows // BLOCK
    first = tokens // 2 - length // 2
    n0, n1 = first // length, (first + SECOND) // length
    reach = min(max(n0, n1 - n0, n_ctx - n1), n_ctx - 1)
    hbm = pl.BlockSpec(memory_space=pltpu.HBM)
    vmem = pl.BlockSpec(memory_space=pltpu.VMEM)
    dma, plain = pltpu.SemaphoreType.DMA, pltpu.SemaphoreType.REGULAR
    others = max(n_head - 1, 1)
    operands = (
        queries, keys, values,
        q_feature.transpose(0, 2, 1), k_feature[0].T,
        doc_lengths.reshape(1, -1),
    )
    parts = pl.pallas_call(
        functools.partial(kernel, n_ctx, n_head, n0, n1, reach),
        out_shape=[
            jax.ShapeDtypeStruct((blocks, hd + ZROWS, BLOCK), BF16),
            jax.ShapeDtypeStruct((blocks, hd + ZROWS, 2 * half), BF16),
            jax.ShapeDtypeStruct((blocks, BLOCK + 2 * half, heads * BLOCK), BF16),
            jax.ShapeDtypeStruct((length, heads * hd), BF16),
        ],
        in_specs=[hbm] * 6,
        out_specs=[vmem] * 4,
        scratch_shapes=[
            pltpu.VMEM((n_head, rows, heads * hd), BF16),
            pltpu.VMEM((n_head, rows, hd), BF16),
            pltpu.VMEM((length, hd), BF16),
            pltpu.VMEM((n_head, heads, half, hd), BF16),
            pltpu.VMEM((n_head, half, hd), BF16),
            pltpu.VMEM((1, doc_lengths.shape[0]), jnp.int32),
            pltpu.VMEM((others, half, rows), BF16),
            pltpu.VMEM((others, per, heads * half, BLOCK), BF16),
            pltpu.VMEM((others, half, rows), BF16),
            pltpu.VMEM((others, per, heads * half, BLOCK), BF16),
            pltpu.VMEM((blocks, BLOCK, 2 * half), BF16),
            pltpu.VMEM((per, 2 * half, heads * BLOCK), BF16),
            pltpu.VMEM((blocks + 1, hd + ZROWS, 2 * half), F32),
            pltpu.VMEM((blocks, hd + ZROWS, 2 * half), F32),
            pltpu.VMEM((blocks, 8, BLOCK), F32),
            pltpu.VMEM((hd + ZROWS, 2 * half), BF16),
            pltpu.VMEM((reach, hd + ZROWS, 2 * half), BF16),
            dma((4 + 2 * n_head,)),
            dma((others, 2)),
            dma((others, 2)),
            dma((others, 2)),
            dma((others, 2)),
            dma((others, per)),
            dma((others, per)),
            dma((reach,)),
            dma((reach,)),
            plain, plain, plain, plain,
        ],
        compiler_params=pltpu.CompilerParams(
            collective_id=0, has_side_effects=True, vmem_limit_bytes=32 << 20
        ),
    )(*[pltpu.with_memory_space_constraint(a, pltpu.HBM) for a in operands])
    return pl.pallas_call(
        functools.partial(last_kernel, n_ctx, n_head, n0, n1),
        out_shape=jax.ShapeDtypeStruct((length, heads * hd), BF16),
        in_specs=[vmem] * 4,
        out_specs=hbm,
        scratch_shapes=[pltpu.VMEM((length, heads * hd), BF16), dma((blocks,))],
        compiler_params=pltpu.CompilerParams(vmem_limit_bytes=32 << 20),
    )(*parts)


def solution(mesh):
    placed = (
        P(("ctx", "head"), None),
        P(("ctx", "head"), None),
        P(("ctx", "head"), None),
        P("head", None, None),
        P("head", None, None),
        P(),
    )
    return jax.shard_map(
        functools.partial(body, mesh.shape["ctx"], mesh.shape["head"]),
        mesh=mesh,
        in_specs=placed,
        out_specs=P("ctx", "head"),
        check_vma=False,
    )
```

```python
import functools

import jax
import jax.numpy as jnp
from jax import lax
from jax.experimental import pallas as pl
from jax.experimental.pallas import tpu as pltpu
from jax.sharding import PartitionSpec as P

MESH = pl.DeviceIdType.MESH
F32 = jnp.float32
BF16 = jnp.bfloat16
NT = (((1,), (1,)), ((), ()))
SECOND = 3 * 1024
ZROWS = 16
BLOCK = 128
SPAN = 80.0
EARLY = 1


def iota(shape, dim):
    return lax.broadcasted_iota(jnp.int32, shape, dim)


def extremes(p):
    return jnp.max(p, 0, keepdims=True), jnp.min(p, 0, keepdims=True)


def features(p):
    top, low = extremes(p)
    up, down = jnp.exp(p - top), jnp.exp(low - p)
    up = up * (1.0 / jnp.sum(up, 0, keepdims=True))
    down = down * (1.0 / jnp.sum(down, 0, keepdims=True))
    return jnp.concatenate([up, down], 0)


def encode(p):
    top, low = extremes(p)
    reach = jnp.minimum(SPAN, 0.5 * (top - low))
    return jnp.exp(jnp.maximum(p - top + reach, 0.0) + jnp.minimum(p - low - reach, 0.0)).astype(BF16)


def decode(u):
    up = u.astype(F32)
    down = 1.0 / up
    up = up * (1.0 / jnp.sum(up, 0, keepdims=True))
    down = down * (1.0 / jnp.sum(down, 0, keepdims=True))
    return jnp.concatenate([up, down], 0)


def span(n_ctx, n0, n1, b):
    def last_of(j):
        return jnp.where(j < n0, n0 - 1, jnp.where(j < n1, n1 - 1, n_ctx - 1))

    def first_of(j):
        return jnp.where(j < n0, 0, jnp.where(j < n1, n0, n1))

    return jnp.minimum(last_of(b) + 1, n_ctx - 1) - b, jnp.where(b == 0, 0, b - first_of(b - 1))


def token_rows(i, n=1):
    if isinstance(i, int):
        return pl.ds(i * BLOCK, n * BLOCK)
    return pl.ds(pl.multiple_of(i * BLOCK, BLOCK), n * BLOCK)


def finish(c, v_ext, held, mixed, out):
    hd = BLOCK
    left = jnp.concatenate([v_ext[c], held[c]], 1)
    for p in range(mixed.shape[1]):
        acc = jnp.dot(left, mixed[c, p], preferred_element_type=F32)
        done = (acc[:hd] * (1.0 / acc[hd : hd + 1])).astype(BF16)
        for m in range(2):
            h = 2 * p + m
            out[token_rows(c), h * hd : (h + 1) * hd] = done[:, m * hd : (m + 1) * hd].T


def kernel(
    n_ctx, n_head, n0, n1, reach,
    q_hbm, k_hbm, v_hbm, wq_hbm, wk_hbm, len_hbm, v_ext, held, mixed, out,
    xq, xk, v_buf, wq_buf, wk_buf, len_ref,
    uk_out, uq_out, uk_in, uq_in, phi_k, phi_q, carry, fresh, lo_ref, state_out, state_in,
    load_sem, w_send, w_recv, f_send, f_recv, kv_send, kv_recv, q_send, q_recv, s_send, s_recv,
    here_sem, all_sem, ctx_sem, turn_sem,
):
    me, b = lax.axis_index("head"), lax.axis_index("ctx")
    rows, hd = q_hbm.shape[0], BLOCK
    heads = wq_hbm.shape[0]
    half = hd // 2
    wide = heads * hd
    blocks = phi_k.shape[0]
    per = rows // BLOCK
    step = min(2, per)
    units = 2 * per
    hold = units - 2 if per >= 4 else units
    length = blocks * BLOCK
    begin = b * length
    others = range(1, n_head)
    second = lax.rem(b, 2)

    def pair(turn):
        return lax.rem(second + turn, 2)

    def pair_heads(turn):
        return pl.ds(2 * pair(turn), 2)

    def peer(o):
        return lax.rem(me + o, n_head)

    n_to, n_from = span(n_ctx, n0, n1, b)
    early = n_from <= EARLY

    barrier = pltpu.get_barrier_semaphore()

    @pl.when(me == 0)
    def _():
        for o in others:
            pl.semaphore_signal(barrier, inc=1, device_id=(b, o), device_id_type=MESH)

    own = pl.ds(pl.multiple_of(me * rows, rows), rows)

    def q_cols(o):
        return pl.ds(pl.multiple_of(peer(o) * wide, wide), wide)

    def kv_cols(o):
        return pl.ds(pl.multiple_of(peer(o) * hd, hd), hd)

    small = [
        pltpu.make_async_copy(src, dst, load_sem.at[i])
        for i, (src, dst) in enumerate(
            ((len_hbm, len_ref), (wk_hbm, wk_buf.at[0]), (wq_hbm, wq_buf.at[0]))
        )
    ]
    k_load = [
        pltpu.make_async_copy(k_hbm.at[:, kv_cols(o)], xk.at[o], load_sem.at[4 + o])
        for o in range(n_head)
    ]
    v_load = pltpu.make_async_copy(v_hbm.at[:, kv_cols(0)], v_buf.at[own, :], load_sem.at[3])
    q_load = [
        pltpu.make_async_copy(q_hbm.at[:, q_cols(o)], xq.at[o], load_sem.at[4 + n_head + o])
        for o in range(n_head)
    ]
    @pl.when(me == 0)
    def _():
        for c in (*small, *k_load, v_load, *q_load):
            c.start()

    @pl.when(me != 0)
    def _():
        pl.semaphore_wait(barrier, 1)
        pl.semaphore_signal(here_sem, inc=1, device_id=(b, 0), device_id_type=MESH)

    @pl.when(me == 0)
    def _():
        pl.semaphore_wait(here_sem, n_head - 1)

    if n_head > 2:

        @pl.when(me == 0)
        def _():
            for o in others:
                pl.semaphore_signal(all_sem, inc=1, device_id=(b, o), device_id_type=MESH)

        @pl.when(me != 0)
        def _():
            pl.semaphore_wait(all_sem, 1)

    def remote(src, dst, send, recv, o):
        return pltpu.make_async_remote_copy(
            src_ref=src, dst_ref=dst, send_sem=send, recv_sem=recv,
            device_id=(b, peer(o)), device_id_type=MESH,
        )

    def w_copy(o, which):
        slot = n_head - o
        src, dst = (
            (wk_hbm, wk_buf.at[slot]),
            (wq_hbm.at[pair_heads(0)], wq_buf.at[slot, pair_heads(0)]),
        )[which]
        return remote(src, dst, w_send.at[slot - 1, which], w_recv.at[slot - 1, which], o)

    def w_pass(o):
        place = wq_buf.at[o, pair_heads(0)]
        return pltpu.make_async_remote_copy(
            src_ref=place, dst_ref=place, send_sem=f_send.at[o - 1], recv_sem=f_recv.at[o - 1],
            device_id=(b + 1 - 2 * second, me), device_id_type=MESH,
        )

    def v_copy(o):
        slot = n_head - o - 1
        return remote(
            v_hbm.at[:, kv_cols(o)], v_buf.at[own, :], kv_send.at[slot, 0], kv_recv.at[slot, 0], o
        )

    def k_copy(o):
        slot = n_head - o - 1
        return remote(
            uk_out.at[slot], uk_in.at[slot], kv_send.at[slot, 1], kv_recv.at[slot, 1], o
        )

    def q_copy(o, n):
        slot = n_head - o - 1
        return remote(
            uq_out.at[slot, n], uq_in.at[slot, n], q_send.at[slot, n], q_recv.at[slot, n], o
        )

    for o in others:
        w_copy(o, 0).start()
        w_copy(o, 1).start()
    for o in others:
        v_copy(o).start()

    @pl.when(me != 0)
    def _():
        for c in (*small, *k_load, v_load, *q_load):
            c.start()

    @pl.when(me == 0)
    def _():
        def greet(i, _):
            @pl.when(i <= n_to)
            def _():
                pl.semaphore_signal(barrier, inc=1, device_id=(b + i, 0), device_id_type=MESH)

            @pl.when(i <= n_from)
            def _():
                pl.semaphore_signal(barrier, inc=1, device_id=(b - i, 0), device_id_type=MESH)

            return 0

        lax.fori_loop(1, reach + 1, greet, 0)

    for c in small:
        c.wait()
    docs = len_ref.shape[1]
    lens = jnp.broadcast_to(len_ref[...].astype(F32), (docs, docs))
    starts = jnp.sum(
        jnp.where(iota((docs, docs), 1) < iota((docs, docs), 0), lens, 0.0), 1, keepdims=True
    )

    def doc_start(pos):
        return jnp.max(jnp.where(starts <= pos, starts, -1.0), 0, keepdims=True)

    lane = iota((1, BLOCK), 1)
    for c in range(blocks):
        pos = (begin + c * BLOCK + lane).astype(F32)
        lo_ref[c] = jnp.broadcast_to(doc_start(pos), (8, BLOCK))
    v_ext[:, hd:, :] = jnp.ones((blocks, ZROWS, BLOCK), BF16)

    def pair_weights(o, p):
        zero = jnp.zeros((half, hd), BF16)
        return jnp.concatenate(
            [
                jnp.concatenate([wq_buf[o, 2 * p], zero], 1),
                jnp.concatenate([zero, wq_buf[o, 2 * p + 1]], 1),
            ],
            0,
        )

    def project(o, p, w, i):
        cols = pl.ds(pl.multiple_of(2 * p * hd, 2 * hd), 2 * hd)
        x = xq[o, token_rows(i * step, step), cols]
        return lax.dot_general(w, x, NT, preferred_element_type=F32)

    def edge_at(pos):
        return doc_start(pos.astype(F32))

    def set_values(c):
        v_ext[c, :hd, :] = v_buf[token_rows(c), :].T

    def set_keys(c, phi):
        keys = phi.astype(BF16).T
        phi_k[c] = keys
        c0 = begin + c * BLOCK
        chosen = ((c0 + lane).astype(F32) >= edge_at(c0 + BLOCK - 1)).astype(F32).astype(BF16)
        fresh[c] = jnp.dot(v_ext[c] * chosen, keys, preferred_element_type=F32)

    k_load[0].wait()
    v_load.wait()

    def own_keys(i, _):
        p = lax.dot_general(
            wk_buf[0], xk[0, token_rows(i * step, step), :], NT, preferred_element_type=F32
        )
        phi = features(p)
        for j in range(step):
            set_values(me * per + i * step + j)
            set_keys(me * per + i * step + j, phi[:, j * BLOCK : (j + 1) * BLOCK])
        return 0

    lax.fori_loop(0, per // step, own_keys, 0, unroll=True)
    q_load[0].wait()
    weights = [pair_weights(0, p) for p in range(2)]

    def own_queries(i, _):
        for p, w in enumerate(weights):
            projected = project(0, p, w, i)
            for m in range(2):
                phi = features(projected[m * half : (m + 1) * half]).astype(BF16)
                for j in range(step):
                    phi_q[i * step + j, p, :, m * hd : (m + 1) * hd] = phi[
                        :, j * BLOCK : (j + 1) * BLOCK
                    ]
        return 0

    lax.fori_loop(0, per // step, own_queries, 0, unroll=True)

    for o in others:
        w_copy(n_head - o, 0).wait_recv()
        k_load[o].wait()
        p = lax.dot_general(wk_buf[o], xk[o], NT, preferred_element_type=F32)
        uk_out[n_head - o - 1] = encode(p)
        k_copy(o).start()
    def send_queries(o, turn):
        w = pair_weights(o, pair(turn))
        for i in range(per // step):
            projected = project(o, pair(turn), w, i)
            for m in range(2):
                u = encode(projected[m * half : (m + 1) * half])
                for j in range(step):
                    n = turn * per + i * step + j
                    uq_out[n_head - o - 1, n, m * half : (m + 1) * half, :] = u[
                        :, j * BLOCK : (j + 1) * BLOCK
                    ]
            for j in range(step):
                n = turn * per + i * step + j
                if n < hold:
                    q_copy(o, n).start()
                else:

                    @pl.when(second == 0)
                    def _(copy=q_copy(o, n)):
                        copy.start()

    for o in others:
        w_copy(n_head - o, 1).wait_recv()
        q_load[o].wait()
        send_queries(o, 0)

    @pl.when(me == 0)
    def _():
        pl.semaphore_wait(barrier, n_to + n_from)
        for o in others:
            pl.semaphore_signal(ctx_sem, inc=1, device_id=(b, o), device_id_type=MESH)

    @pl.when(me != 0)
    def _():
        pl.semaphore_wait(ctx_sem, 1)

    for o in others:
        w_pass(o).start()
    for o in others:
        w_pass(o).wait_recv()
        send_queries(o, 1)

    within = [edge_at(begin + (c + 1) * BLOCK - 1) < (begin + c * BLOCK).astype(F32) for c in range(blocks)]
    across = [edge_at(begin + c * BLOCK - 1) < begin.astype(F32) for c in range(blocks)]
    before = edge_at(begin - 1)
    for o in others:
        v_copy(n_head - o).wait_recv()
        for i in range(per):
            set_values(peer(o) * per + i)
    for o in others:
        k_copy(n_head - o).wait_recv()
        phi = decode(uk_in[o - 1])
        for i in range(per):
            set_keys(peer(o) * per + i, phi[:, i * BLOCK : (i + 1) * BLOCK])

    total = jnp.zeros((hd + ZROWS, hd), F32)
    for c in range(blocks):
        carry[c] = total
        total = fresh[c] + jnp.where(within[c], total, 0.0)
    state_out[...] = total.astype(BF16)

    def s_copy(i):
        return pltpu.make_async_remote_copy(
            src_ref=state_out,
            dst_ref=state_in.at[i - 1],
            send_sem=s_send.at[i - 1],
            recv_sem=s_recv.at[i - 1],
            device_id=(b + i, me),
            device_id_type=MESH,
        )

    def push(i, _):
        @pl.when(i <= n_to)
        def _():
            s_copy(i).start()

        return 0

    lax.fori_loop(1, reach + 1, push, 0)

    if hold < units:

        @pl.when(second == 0)
        def _():
            for o in others:
                q_copy(o, hold - 3).wait_send()
            pl.semaphore_signal(turn_sem, inc=1, device_id=(b + 1, me), device_id_type=MESH)

        @pl.when(second == 1)
        def _():
            pl.semaphore_wait(turn_sem, 1)
            for o in others:
                for n in range(hold, units):
                    q_copy(o, n).start()


    def weigh(c, p, q):
        c0 = begin + c * BLOCK
        scores = jnp.dot(phi_k[c], q, preferred_element_type=F32)
        lo = lo_ref[c, 0:1, :]
        s_i = iota((BLOCK, BLOCK), 0)
        mask = (s_i <= iota((BLOCK, BLOCK), 1)) & ((c0 + s_i).astype(F32) >= lo)
        carried = (lo < c0.astype(F32)).astype(F32).astype(BF16)
        for m in range(2):
            cols = slice(m * hd, (m + 1) * hd)
            mixed[c, p, :BLOCK, cols] = jnp.where(mask, scores[:, cols], 0.0).astype(BF16)
        mixed[c, p, BLOCK:, :] = q * jnp.concatenate([carried] * 2, 1)

    def weigh_sent(o, n):
        q_copy(n_head - o, n).wait_recv()
        u = uq_in[o - 1, n]
        q = jnp.concatenate(
            [decode(u[m * half : (m + 1) * half]).astype(BF16) for m in range(2)], 1
        )
        weigh(peer(o) * per + n % per, pair(n // per), q)

    def collect(i, _):
        @pl.when(i <= n_from)
        def _():
            s_copy(i).wait_recv()
            end = ((b - i + 1) * length - 1).astype(F32)
            carry[blocks] += jnp.where(end >= before, state_in[i - 1].astype(F32), 0.0)

        return 0

    def enter():
        carry[blocks] = jnp.zeros((hd + ZROWS, hd), F32)
        lax.fori_loop(1, reach + 1, collect, 0)
        for c in range(blocks):
            held[c] = (carry[c] + jnp.where(across[c], carry[blocks], 0.0)).astype(BF16)

    order = [(o, n) for o in others for n in range(units)]
    for i in range(per):
        for p in range(2):
            weigh(me * per + i, p, phi_q[i, p])
    for o, n in order[:-1]:
        weigh_sent(o, n)

    @pl.when(early)
    def _():
        enter()
        for o, i in [(o, i) for o in range(n_head) for i in range(per)][:-1]:
            finish(peer(o) * per + i, v_ext, held, mixed, out)

    for o in others:
        w_copy(o, 0).wait_send()
        w_copy(o, 1).wait_send()
        v_copy(o).wait_send()
        k_copy(o).wait_send()
        w_pass(o).wait_send()
        for n in range(units):
            if hold < units and n == hold - 3:

                @pl.when(second == 1)
                def _(copy=q_copy(o, n)):
                    copy.wait_send()

            else:
                q_copy(o, n).wait_send()

    def pushed(i, _):
        @pl.when(i <= n_to)
        def _():
            s_copy(i).wait_send()

        return 0

    lax.fori_loop(1, reach + 1, pushed, 0)

    weigh_sent(*order[-1])

    @pl.when(jnp.logical_not(early))
    def _():
        enter()


def last_kernel(n_ctx, n_head, n0, n1, v_ext, held, mixed, made, out_hbm, out, out_sem):
    me, b = lax.axis_index("head"), lax.axis_index("ctx")
    blocks = mixed.shape[0]
    per = blocks // n_head
    early = span(n_ctx, n0, n1, b)[1] <= EARLY
    last = lax.rem(me + n_head - 1, n_head) * per + per - 1

    def write(c, src):
        rows = token_rows(c)
        return pltpu.make_async_copy(src.at[rows], out_hbm.at[rows], out_sem.at[c])

    @pl.when(early)
    def _():
        for c in range(blocks):

            @pl.when(c != last)
            def _(c=c):
                write(c, made).start()

        finish(last, v_ext, held, mixed, out)
        write(last, out).start()

    @pl.when(jnp.logical_not(early))
    def _():
        for c in range(blocks):
            finish(c, v_ext, held, mixed, out)
            write(c, out).start()

    for c in range(blocks):
        write(c, out).wait()


def body(n_ctx, n_head, queries, keys, values, q_feature, k_feature, doc_lengths):
    rows = queries.shape[0]
    heads, hd, half = q_feature.shape
    length = rows * n_head
    tokens = length * n_ctx
    blocks = length // BLOCK
    per = rows // BLOCK
    first = tokens // 2 - length // 2
    n0, n1 = first // length, (first + SECOND) // length
    reach = min(max(n0, n1 - n0, n_ctx - n1), n_ctx - 1)
    hbm = pl.BlockSpec(memory_space=pltpu.HBM)
    vmem = pl.BlockSpec(memory_space=pltpu.VMEM)
    dma, plain = pltpu.SemaphoreType.DMA, pltpu.SemaphoreType.REGULAR
    others = max(n_head - 1, 1)
    operands = (
        queries, keys, values,
        q_feature.transpose(0, 2, 1), k_feature[0].T,
        doc_lengths.reshape(1, -1),
    )
    parts = pl.pallas_call(
        functools.partial(kernel, n_ctx, n_head, n0, n1, reach),
        out_shape=[
            jax.ShapeDtypeStruct((blocks, hd + ZROWS, BLOCK), BF16),
            jax.ShapeDtypeStruct((blocks, hd + ZROWS, 2 * half), BF16),
            jax.ShapeDtypeStruct((blocks, heads // 2, BLOCK + 2 * half, 2 * BLOCK), BF16),
            jax.ShapeDtypeStruct((length, heads * hd), BF16),
        ],
        in_specs=[hbm] * 6,
        out_specs=[vmem] * 4,
        scratch_shapes=[
            pltpu.VMEM((n_head, rows, heads * hd), BF16),
            pltpu.VMEM((n_head, rows, hd), BF16),
            pltpu.VMEM((length, hd), BF16),
            pltpu.VMEM((n_head, heads, half, hd), BF16),
            pltpu.VMEM((n_head, half, hd), BF16),
            pltpu.VMEM((1, doc_lengths.shape[0]), jnp.int32),
            pltpu.VMEM((others, half, rows), BF16),
            pltpu.VMEM((others, 2 * per, 2 * half, BLOCK), BF16),
            pltpu.VMEM((others, half, rows), BF16),
            pltpu.VMEM((others, 2 * per, 2 * half, BLOCK), BF16),
            pltpu.VMEM((blocks, BLOCK, 2 * half), BF16),
            pltpu.VMEM((per, heads // 2, 2 * half, 2 * BLOCK), BF16),
            pltpu.VMEM((blocks + 1, hd + ZROWS, 2 * half), F32),
            pltpu.VMEM((blocks, hd + ZROWS, 2 * half), F32),
            pltpu.VMEM((blocks, 8, BLOCK), F32),
            pltpu.VMEM((hd + ZROWS, 2 * half), BF16),
            pltpu.VMEM((reach, hd + ZROWS, 2 * half), BF16),
            dma((4 + 2 * n_head,)),
            dma((others, 2)),
            dma((others, 2)),
            dma((others,)),
            dma((others,)),
            dma((others, 2)),
            dma((others, 2)),
            dma((others, 2 * per)),
            dma((others, 2 * per)),
            dma((reach,)),
            dma((reach,)),
            plain, plain, plain, plain,
        ],
        compiler_params=pltpu.CompilerParams(
            collective_id=0, has_side_effects=True, vmem_limit_bytes=32 << 20
        ),
    )(*[pltpu.with_memory_space_constraint(a, pltpu.HBM) for a in operands])
    return pl.pallas_call(
        functools.partial(last_kernel, n_ctx, n_head, n0, n1),
        out_shape=jax.ShapeDtypeStruct((length, heads * hd), BF16),
        in_specs=[vmem] * 4,
        out_specs=hbm,
        scratch_shapes=[pltpu.VMEM((length, heads * hd), BF16), dma((blocks,))],
        compiler_params=pltpu.CompilerParams(vmem_limit_bytes=32 << 20),
    )(*parts)


def solution(mesh):
    placed = (
        P(("ctx", "head"), None),
        P(("ctx", "head"), None),
        P(("ctx", "head"), None),
        P("head", None, None),
        P("head", None, None),
        P(),
    )
    return jax.shard_map(
        functools.partial(body, mesh.shape["ctx"], mesh.shape["head"]),
        mesh=mesh,
        in_specs=placed,
        out_specs=P("ctx", "head"),
        check_vma=False,
    )
```

```python
import functools

import jax
import jax.numpy as jnp
from jax import lax
from jax.experimental import pallas as pl
from jax.experimental.pallas import tpu as pltpu
from jax.sharding import PartitionSpec as P

MESH = pl.DeviceIdType.MESH
F32 = jnp.float32
BF16 = jnp.bfloat16
NT = (((1,), (1,)), ((), ()))
SECOND = 3 * 1024
ZROWS = 16
BLOCK = 128
SPAN = 80.0
EARLY = 1


def iota(shape, dim):
    return lax.broadcasted_iota(jnp.int32, shape, dim)


def extremes(p):
    return jnp.max(p, 0, keepdims=True), jnp.min(p, 0, keepdims=True)


def features(p):
    top, low = extremes(p)
    up, down = jnp.exp(p - top), jnp.exp(low - p)
    up = up * (1.0 / jnp.sum(up, 0, keepdims=True))
    down = down * (1.0 / jnp.sum(down, 0, keepdims=True))
    return jnp.concatenate([up, down], 0)


def encode(p):
    top, low = extremes(p)
    reach = jnp.minimum(SPAN, 0.5 * (top - low))
    return jnp.exp(jnp.maximum(p - top + reach, 0.0) + jnp.minimum(p - low - reach, 0.0)).astype(BF16)


def decode(u):
    up = u.astype(F32)
    down = 1.0 / up
    up = up * (1.0 / jnp.sum(up, 0, keepdims=True))
    down = down * (1.0 / jnp.sum(down, 0, keepdims=True))
    return jnp.concatenate([up, down], 0)


def span(n_ctx, n0, n1, b):
    def last_of(j):
        return jnp.where(j < n0, n0 - 1, jnp.where(j < n1, n1 - 1, n_ctx - 1))

    def first_of(j):
        return jnp.where(j < n0, 0, jnp.where(j < n1, n0, n1))

    return jnp.minimum(last_of(b) + 1, n_ctx - 1) - b, jnp.where(b == 0, 0, b - first_of(b - 1))


def token_rows(i, n=1):
    if isinstance(i, int):
        return pl.ds(i * BLOCK, n * BLOCK)
    return pl.ds(pl.multiple_of(i * BLOCK, BLOCK), n * BLOCK)


def finish(c, v_ext, held, mixed, out):
    hd = BLOCK
    left = jnp.concatenate([v_ext[c], held[c]], 1)
    for p in range(mixed.shape[1]):
        acc = jnp.dot(left, mixed[c, p], preferred_element_type=F32)
        done = (acc[:hd] * (1.0 / acc[hd : hd + 1])).astype(BF16)
        for m in range(2):
            h = 2 * p + m
            out[token_rows(c), h * hd : (h + 1) * hd] = done[:, m * hd : (m + 1) * hd].T


def kernel(
    n_ctx, n_head, n0, n1, reach,
    q_hbm, k_hbm, v_hbm, wq_hbm, wk_hbm, len_hbm, v_ext, held, mixed, out,
    xq, xk, v_buf, wq_buf, wk_buf, len_ref,
    uk_out, uq_out, uk_in, uq_in, phi_k, phi_q, carry, fresh, lo_ref, state_out, state_in,
    load_sem, w_send, w_recv, f_send, f_recv, kv_send, kv_recv, q_send, q_recv, s_send, s_recv,
    here_sem, all_sem, ctx_sem, turn_sem,
):
    me, b = lax.axis_index("head"), lax.axis_index("ctx")
    rows, hd = q_hbm.shape[0], BLOCK
    heads = wq_hbm.shape[0]
    half = hd // 2
    wide = heads * hd
    blocks = phi_k.shape[0]
    per = rows // BLOCK
    step = min(2, per)
    units = 2 * per
    hold = units - 3 if per >= 4 else units
    length = blocks * BLOCK
    begin = b * length
    others = range(1, n_head)
    second = lax.rem(b, 2)

    def pair(turn):
        return lax.rem(second + turn, 2)

    def pair_heads(turn):
        return pl.ds(2 * pair(turn), 2)

    def peer(o):
        return lax.rem(me + o, n_head)

    n_to, n_from = span(n_ctx, n0, n1, b)
    early = n_from <= EARLY

    barrier = pltpu.get_barrier_semaphore()

    @pl.when(me == 0)
    def _():
        for o in others:
            pl.semaphore_signal(barrier, inc=1, device_id=(b, o), device_id_type=MESH)

    own = pl.ds(pl.multiple_of(me * rows, rows), rows)

    def q_cols(o):
        return pl.ds(pl.multiple_of(peer(o) * wide, wide), wide)

    def kv_cols(o):
        return pl.ds(pl.multiple_of(peer(o) * hd, hd), hd)

    small = [
        pltpu.make_async_copy(src, dst, load_sem.at[i])
        for i, (src, dst) in enumerate(
            ((len_hbm, len_ref), (wk_hbm, wk_buf.at[0]), (wq_hbm, wq_buf.at[0]))
        )
    ]
    k_load = [
        pltpu.make_async_copy(k_hbm.at[:, kv_cols(o)], xk.at[o], load_sem.at[4 + o])
        for o in range(n_head)
    ]
    v_load = pltpu.make_async_copy(v_hbm.at[:, kv_cols(0)], v_buf.at[own, :], load_sem.at[3])
    q_load = [
        pltpu.make_async_copy(q_hbm.at[:, q_cols(o)], xq.at[o], load_sem.at[4 + n_head + o])
        for o in range(n_head)
    ]
    @pl.when(me == 0)
    def _():
        for c in (*small, *k_load, v_load, *q_load):
            c.start()

    @pl.when(me != 0)
    def _():
        pl.semaphore_wait(barrier, 1)
        pl.semaphore_signal(here_sem, inc=1, device_id=(b, 0), device_id_type=MESH)

    @pl.when(me == 0)
    def _():
        pl.semaphore_wait(here_sem, n_head - 1)

    if n_head > 2:

        @pl.when(me == 0)
        def _():
            for o in others:
                pl.semaphore_signal(all_sem, inc=1, device_id=(b, o), device_id_type=MESH)

        @pl.when(me != 0)
        def _():
            pl.semaphore_wait(all_sem, 1)

    def remote(src, dst, send, recv, o):
        return pltpu.make_async_remote_copy(
            src_ref=src, dst_ref=dst, send_sem=send, recv_sem=recv,
            device_id=(b, peer(o)), device_id_type=MESH,
        )

    def w_copy(o, which):
        slot = n_head - o
        src, dst = (
            (wk_hbm, wk_buf.at[slot]),
            (wq_hbm.at[pair_heads(0)], wq_buf.at[slot, pair_heads(0)]),
        )[which]
        return remote(src, dst, w_send.at[slot - 1, which], w_recv.at[slot - 1, which], o)

    def w_pass(o):
        place = wq_buf.at[o, pair_heads(0)]
        return pltpu.make_async_remote_copy(
            src_ref=place, dst_ref=place, send_sem=f_send.at[o - 1], recv_sem=f_recv.at[o - 1],
            device_id=(b + 1 - 2 * second, me), device_id_type=MESH,
        )

    def v_copy(o):
        slot = n_head - o - 1
        return remote(
            v_hbm.at[:, kv_cols(o)], v_buf.at[own, :], kv_send.at[slot, 0], kv_recv.at[slot, 0], o
        )

    def k_copy(o):
        slot = n_head - o - 1
        return remote(
            uk_out.at[slot], uk_in.at[slot], kv_send.at[slot, 1], kv_recv.at[slot, 1], o
        )

    def q_copy(o, n):
        slot = n_head - o - 1
        return remote(
            uq_out.at[slot, n], uq_in.at[slot, n], q_send.at[slot, n], q_recv.at[slot, n], o
        )

    for o in others:
        w_copy(o, 0).start()
        w_copy(o, 1).start()
    for o in others:
        v_copy(o).start()

    @pl.when(me != 0)
    def _():
        for c in (*small, *k_load, v_load, *q_load):
            c.start()

    @pl.when(me == 0)
    def _():
        def greet(i, _):
            @pl.when(i <= n_to)
            def _():
                pl.semaphore_signal(barrier, inc=1, device_id=(b + i, 0), device_id_type=MESH)

            @pl.when(i <= n_from)
            def _():
                pl.semaphore_signal(barrier, inc=1, device_id=(b - i, 0), device_id_type=MESH)

            return 0

        lax.fori_loop(1, reach + 1, greet, 0)

    for c in small:
        c.wait()
    docs = len_ref.shape[1]
    lens = jnp.broadcast_to(len_ref[...].astype(F32), (docs, docs))
    starts = jnp.sum(
        jnp.where(iota((docs, docs), 1) < iota((docs, docs), 0), lens, 0.0), 1, keepdims=True
    )

    def doc_start(pos):
        return jnp.max(jnp.where(starts <= pos, starts, -1.0), 0, keepdims=True)

    lane = iota((1, BLOCK), 1)
    for c in range(blocks):
        pos = (begin + c * BLOCK + lane).astype(F32)
        lo_ref[c] = jnp.broadcast_to(doc_start(pos), (8, BLOCK))
    v_ext[:, hd:, :] = jnp.ones((blocks, ZROWS, BLOCK), BF16)

    def pair_weights(o, p):
        zero = jnp.zeros((half, hd), BF16)
        return jnp.concatenate(
            [
                jnp.concatenate([wq_buf[o, 2 * p], zero], 1),
                jnp.concatenate([zero, wq_buf[o, 2 * p + 1]], 1),
            ],
            0,
        )

    def project(o, p, w, i):
        cols = pl.ds(pl.multiple_of(2 * p * hd, 2 * hd), 2 * hd)
        x = xq[o, token_rows(i * step, step), cols]
        return lax.dot_general(w, x, NT, preferred_element_type=F32)

    def edge_at(pos):
        return doc_start(pos.astype(F32))

    def set_values(c):
        v_ext[c, :hd, :] = v_buf[token_rows(c), :].T

    def set_keys(c, phi):
        keys = phi.astype(BF16).T
        phi_k[c] = keys
        c0 = begin + c * BLOCK
        chosen = ((c0 + lane).astype(F32) >= edge_at(c0 + BLOCK - 1)).astype(F32).astype(BF16)
        fresh[c] = jnp.dot(v_ext[c] * chosen, keys, preferred_element_type=F32)

    k_load[0].wait()
    v_load.wait()

    def own_keys(i, _):
        p = lax.dot_general(
            wk_buf[0], xk[0, token_rows(i * step, step), :], NT, preferred_element_type=F32
        )
        phi = features(p)
        for j in range(step):
            set_values(me * per + i * step + j)
            set_keys(me * per + i * step + j, phi[:, j * BLOCK : (j + 1) * BLOCK])
        return 0

    lax.fori_loop(0, per // step, own_keys, 0, unroll=True)
    q_load[0].wait()
    weights = [pair_weights(0, p) for p in range(2)]

    def own_queries(i, _):
        for p, w in enumerate(weights):
            projected = project(0, p, w, i)
            for m in range(2):
                phi = features(projected[m * half : (m + 1) * half]).astype(BF16)
                for j in range(step):
                    phi_q[i * step + j, p, :, m * hd : (m + 1) * hd] = phi[
                        :, j * BLOCK : (j + 1) * BLOCK
                    ]
        return 0

    lax.fori_loop(0, per // step, own_queries, 0, unroll=True)

    for o in others:
        w_copy(n_head - o, 0).wait_recv()
        k_load[o].wait()
        p = lax.dot_general(wk_buf[o], xk[o], NT, preferred_element_type=F32)
        uk_out[n_head - o - 1] = encode(p)
        k_copy(o).start()
    def send_queries(o, turn):
        w = pair_weights(o, pair(turn))
        for i in range(per // step):
            projected = project(o, pair(turn), w, i)
            for m in range(2):
                u = encode(projected[m * half : (m + 1) * half])
                for j in range(step):
                    n = turn * per + i * step + j
                    uq_out[n_head - o - 1, n, m * half : (m + 1) * half, :] = u[
                        :, j * BLOCK : (j + 1) * BLOCK
                    ]
            for j in range(step):
                n = turn * per + i * step + j
                if n < hold:
                    q_copy(o, n).start()
                else:

                    @pl.when(second == 0)
                    def _(copy=q_copy(o, n)):
                        copy.start()

    for o in others:
        w_copy(n_head - o, 1).wait_recv()
        q_load[o].wait()
        send_queries(o, 0)

    @pl.when(me == 0)
    def _():
        pl.semaphore_wait(barrier, n_to + n_from)
        for o in others:
            pl.semaphore_signal(ctx_sem, inc=1, device_id=(b, o), device_id_type=MESH)

    @pl.when(me != 0)
    def _():
        pl.semaphore_wait(ctx_sem, 1)

    for o in others:
        w_pass(o).start()
    for o in others:
        w_pass(o).wait_recv()
        send_queries(o, 1)

    within = [edge_at(begin + (c + 1) * BLOCK - 1) < (begin + c * BLOCK).astype(F32) for c in range(blocks)]
    across = [edge_at(begin + c * BLOCK - 1) < begin.astype(F32) for c in range(blocks)]
    before = edge_at(begin - 1)
    for o in others:
        v_copy(n_head - o).wait_recv()
        for i in range(per):
            set_values(peer(o) * per + i)
    for o in others:
        k_copy(n_head - o).wait_recv()
        phi = decode(uk_in[o - 1])
        for i in range(per):
            set_keys(peer(o) * per + i, phi[:, i * BLOCK : (i + 1) * BLOCK])

    total = jnp.zeros((hd + ZROWS, hd), F32)
    for c in range(blocks):
        carry[c] = total
        total = fresh[c] + jnp.where(within[c], total, 0.0)
    state_out[...] = total.astype(BF16)

    def s_copy(i):
        return pltpu.make_async_remote_copy(
            src_ref=state_out,
            dst_ref=state_in.at[i - 1],
            send_sem=s_send.at[i - 1],
            recv_sem=s_recv.at[i - 1],
            device_id=(b + i, me),
            device_id_type=MESH,
        )

    def push(i, _):
        @pl.when(i <= n_to)
        def _():
            s_copy(i).start()

        return 0

    lax.fori_loop(1, reach + 1, push, 0)

    if hold < units:

        @pl.when(second == 0)
        def _():
            pl.semaphore_signal(turn_sem, inc=1, device_id=(b + 1, me), device_id_type=MESH)

        @pl.when(second == 1)
        def _():
            pl.semaphore_wait(turn_sem, 1)
            for o in others:
                for n in range(hold, units):
                    q_copy(o, n).start()


    def weigh(c, p, q):
        c0 = begin + c * BLOCK
        scores = jnp.dot(phi_k[c], q, preferred_element_type=F32)
        lo = lo_ref[c, 0:1, :]
        s_i = iota((BLOCK, BLOCK), 0)
        mask = (s_i <= iota((BLOCK, BLOCK), 1)) & ((c0 + s_i).astype(F32) >= lo)
        carried = (lo < c0.astype(F32)).astype(F32).astype(BF16)
        for m in range(2):
            cols = slice(m * hd, (m + 1) * hd)
            mixed[c, p, :BLOCK, cols] = jnp.where(mask, scores[:, cols], 0.0).astype(BF16)
        mixed[c, p, BLOCK:, :] = q * jnp.concatenate([carried] * 2, 1)

    def weigh_sent(o, n):
        q_copy(n_head - o, n).wait_recv()
        u = uq_in[o - 1, n]
        q = jnp.concatenate(
            [decode(u[m * half : (m + 1) * half]).astype(BF16) for m in range(2)], 1
        )
        weigh(peer(o) * per + n % per, pair(n // per), q)

    def collect(i, _):
        @pl.when(i <= n_from)
        def _():
            s_copy(i).wait_recv()
            end = ((b - i + 1) * length - 1).astype(F32)
            carry[blocks] += jnp.where(end >= before, state_in[i - 1].astype(F32), 0.0)

        return 0

    def enter():
        carry[blocks] = jnp.zeros((hd + ZROWS, hd), F32)
        lax.fori_loop(1, reach + 1, collect, 0)
        for c in range(blocks):
            held[c] = (carry[c] + jnp.where(across[c], carry[blocks], 0.0)).astype(BF16)

    order = [(o, n) for o in others for n in range(units)]
    for i in range(per):
        for p in range(2):
            weigh(me * per + i, p, phi_q[i, p])
    todo = []
    for at, (o, n) in enumerate(order[:-1]):
        weigh_sent(o, n)
        if n >= per:
            todo.append((o, n - per))
        if at == 1:
            pl.when(early)(enter)
            todo += [(0, i) for i in range(per)]
        now = todo if at == len(order) - 2 else todo[-2:] if at > 1 else []

        @pl.when(early)
        def _(now=tuple(now)):
            for p, i in now:
                finish(peer(p) * per + i, v_ext, held, mixed, out)

        todo = todo[: len(todo) - len(now)]

    for o in others:
        w_copy(o, 0).wait_send()
        w_copy(o, 1).wait_send()
        v_copy(o).wait_send()
        k_copy(o).wait_send()
        w_pass(o).wait_send()
        for n in range(units):
            q_copy(o, n).wait_send()

    def pushed(i, _):
        @pl.when(i <= n_to)
        def _():
            s_copy(i).wait_send()

        return 0

    lax.fori_loop(1, reach + 1, pushed, 0)

    weigh_sent(*order[-1])

    @pl.when(jnp.logical_not(early))
    def _():
        enter()


def last_kernel(n_ctx, n_head, n0, n1, v_ext, held, mixed, made, out_hbm, out, out_sem):
    me, b = lax.axis_index("head"), lax.axis_index("ctx")
    blocks = mixed.shape[0]
    per = blocks // n_head
    early = span(n_ctx, n0, n1, b)[1] <= EARLY
    last = lax.rem(me + n_head - 1, n_head) * per + per - 1

    def write(c, src):
        rows = token_rows(c)
        return pltpu.make_async_copy(src.at[rows], out_hbm.at[rows], out_sem.at[c])

    @pl.when(early)
    def _():
        for c in range(blocks):

            @pl.when(c != last)
            def _(c=c):
                write(c, made).start()

        finish(last, v_ext, held, mixed, out)
        write(last, out).start()

    @pl.when(jnp.logical_not(early))
    def _():
        for c in range(blocks):
            finish(c, v_ext, held, mixed, out)
            write(c, out).start()

    for c in range(blocks):
        write(c, out).wait()


def body(n_ctx, n_head, queries, keys, values, q_feature, k_feature, doc_lengths):
    rows = queries.shape[0]
    heads, hd, half = q_feature.shape
    length = rows * n_head
    tokens = length * n_ctx
    blocks = length // BLOCK
    per = rows // BLOCK
    first = tokens // 2 - length // 2
    n0, n1 = first // length, (first + SECOND) // length
    reach = min(max(n0, n1 - n0, n_ctx - n1), n_ctx - 1)
    hbm = pl.BlockSpec(memory_space=pltpu.HBM)
    vmem = pl.BlockSpec(memory_space=pltpu.VMEM)
    dma, plain = pltpu.SemaphoreType.DMA, pltpu.SemaphoreType.REGULAR
    others = max(n_head - 1, 1)
    operands = (
        queries, keys, values,
        q_feature.transpose(0, 2, 1), k_feature[0].T,
        doc_lengths.reshape(1, -1),
    )
    parts = pl.pallas_call(
        functools.partial(kernel, n_ctx, n_head, n0, n1, reach),
        out_shape=[
            jax.ShapeDtypeStruct((blocks, hd + ZROWS, BLOCK), BF16),
            jax.ShapeDtypeStruct((blocks, hd + ZROWS, 2 * half), BF16),
            jax.ShapeDtypeStruct((blocks, heads // 2, BLOCK + 2 * half, 2 * BLOCK), BF16),
            jax.ShapeDtypeStruct((length, heads * hd), BF16),
        ],
        in_specs=[hbm] * 6,
        out_specs=[vmem] * 4,
        scratch_shapes=[
            pltpu.VMEM((n_head, rows, heads * hd), BF16),
            pltpu.VMEM((n_head, rows, hd), BF16),
            pltpu.VMEM((length, hd), BF16),
            pltpu.VMEM((n_head, heads, half, hd), BF16),
            pltpu.VMEM((n_head, half, hd), BF16),
            pltpu.VMEM((1, doc_lengths.shape[0]), jnp.int32),
            pltpu.VMEM((others, half, rows), BF16),
            pltpu.VMEM((others, 2 * per, 2 * half, BLOCK), BF16),
            pltpu.VMEM((others, half, rows), BF16),
            pltpu.VMEM((others, 2 * per, 2 * half, BLOCK), BF16),
            pltpu.VMEM((blocks, BLOCK, 2 * half), BF16),
            pltpu.VMEM((per, heads // 2, 2 * half, 2 * BLOCK), BF16),
            pltpu.VMEM((blocks + 1, hd + ZROWS, 2 * half), F32),
            pltpu.VMEM((blocks, hd + ZROWS, 2 * half), F32),
            pltpu.VMEM((blocks, 8, BLOCK), F32),
            pltpu.VMEM((hd + ZROWS, 2 * half), BF16),
            pltpu.VMEM((reach, hd + ZROWS, 2 * half), BF16),
            dma((4 + 2 * n_head,)),
            dma((others, 2)),
            dma((others, 2)),
            dma((others,)),
            dma((others,)),
            dma((others, 2)),
            dma((others, 2)),
            dma((others, 2 * per)),
            dma((others, 2 * per)),
            dma((reach,)),
            dma((reach,)),
            plain, plain, plain, plain,
        ],
        compiler_params=pltpu.CompilerParams(
            collective_id=0, has_side_effects=True, vmem_limit_bytes=32 << 20
        ),
    )(*[pltpu.with_memory_space_constraint(a, pltpu.HBM) for a in operands])
    return pl.pallas_call(
        functools.partial(last_kernel, n_ctx, n_head, n0, n1),
        out_shape=jax.ShapeDtypeStruct((length, heads * hd), BF16),
        in_specs=[vmem] * 4,
        out_specs=hbm,
        scratch_shapes=[pltpu.VMEM((length, heads * hd), BF16), dma((blocks,))],
        compiler_params=pltpu.CompilerParams(vmem_limit_bytes=32 << 20),
    )(*parts)


def solution(mesh):
    placed = (
        P(("ctx", "head"), None),
        P(("ctx", "head"), None),
        P(("ctx", "head"), None),
        P("head", None, None),
        P("head", None, None),
        P(),
    )
    return jax.shard_map(
        functools.partial(body, mesh.shape["ctx"], mesh.shape["head"]),
        mesh=mesh,
        in_specs=placed,
        out_specs=P("ctx", "head"),
        check_vma=False,
    )
```

```python
import functools

import jax
import jax.numpy as jnp
from jax import lax
from jax.experimental import pallas as pl
from jax.experimental.pallas import tpu as pltpu
from jax.sharding import PartitionSpec as P

MESH = pl.DeviceIdType.MESH
F32 = jnp.float32
BF16 = jnp.bfloat16
NT = (((1,), (1,)), ((), ()))
SECOND = 3 * 1024
ZROWS = 16
BLOCK = 128
SPAN = 80.0
EARLY = 1


def iota(shape, dim):
    return lax.broadcasted_iota(jnp.int32, shape, dim)


def extremes(p):
    return jnp.max(p, 0, keepdims=True), jnp.min(p, 0, keepdims=True)


def features(p):
    top, low = extremes(p)
    up, down = jnp.exp(p - top), jnp.exp(low - p)
    up = up * (1.0 / jnp.sum(up, 0, keepdims=True))
    down = down * (1.0 / jnp.sum(down, 0, keepdims=True))
    return jnp.concatenate([up, down], 0)


def encode(p):
    top, low = extremes(p)
    reach = jnp.minimum(SPAN, 0.5 * (top - low))
    return jnp.exp(jnp.maximum(p - top + reach, 0.0) + jnp.minimum(p - low - reach, 0.0)).astype(BF16)


def decode(u):
    up = u.astype(F32)
    down = 1.0 / up
    up = up * (1.0 / jnp.sum(up, 0, keepdims=True))
    down = down * (1.0 / jnp.sum(down, 0, keepdims=True))
    return jnp.concatenate([up, down], 0)


def span(n_ctx, n0, n1, b):
    def last_of(j):
        return jnp.where(j < n0, n0 - 1, jnp.where(j < n1, n1 - 1, n_ctx - 1))

    def first_of(j):
        return jnp.where(j < n0, 0, jnp.where(j < n1, n0, n1))

    return jnp.minimum(last_of(b) + 1, n_ctx - 1) - b, jnp.where(b == 0, 0, b - first_of(b - 1))


def token_rows(i, n=1):
    if isinstance(i, int):
        return pl.ds(i * BLOCK, n * BLOCK)
    return pl.ds(pl.multiple_of(i * BLOCK, BLOCK), n * BLOCK)


def finish(c, v_ext, held, mixed, out):
    hd = BLOCK
    left = jnp.concatenate([v_ext[c], held[c]], 1)
    for p in range(mixed.shape[1]):
        acc = jnp.dot(left, mixed[c, p], preferred_element_type=F32)
        done = (acc[:hd] * (1.0 / acc[hd : hd + 1])).astype(BF16)
        for m in range(2):
            h = 2 * p + m
            out[token_rows(c), h * hd : (h + 1) * hd] = done[:, m * hd : (m + 1) * hd].T


def kernel(
    n_ctx, n_head, n0, n1, reach,
    q_hbm, k_hbm, v_hbm, wq_hbm, wk_hbm, len_hbm, v_ext, held, mixed, out,
    xq, xk, v_buf, wq_buf, wk_buf, len_ref,
    uk_out, uq_out, uk_in, uq_in, phi_k, phi_q, carry, fresh, lo_ref, state_out, state_in,
    load_sem, w_send, w_recv, f_send, f_recv, kv_send, kv_recv, q_send, q_recv, s_send, s_recv,
    here_sem, all_sem, ctx_sem, turn_sem,
):
    me, b = lax.axis_index("head"), lax.axis_index("ctx")
    rows, hd = q_hbm.shape[0], BLOCK
    heads = wq_hbm.shape[0]
    half = hd // 2
    wide = heads * hd
    blocks = phi_k.shape[0]
    per = rows // BLOCK
    step = min(2, per)
    units = 2 * per
    hold = units - 3 if per >= 4 else units
    length = blocks * BLOCK
    begin = b * length
    others = range(1, n_head)
    second = lax.rem(b, 2)

    def pair(turn):
        return lax.rem(second + turn, 2)

    def pair_heads(turn):
        return pl.ds(2 * pair(turn), 2)

    def peer(o):
        return lax.rem(me + o, n_head)

    n_to, n_from = span(n_ctx, n0, n1, b)
    early = n_from <= EARLY

    barrier = pltpu.get_barrier_semaphore()

    @pl.when(me == 0)
    def _():
        for o in others:
            pl.semaphore_signal(barrier, inc=1, device_id=(b, o), device_id_type=MESH)

    own = pl.ds(pl.multiple_of(me * rows, rows), rows)

    def q_cols(o):
        return pl.ds(pl.multiple_of(peer(o) * wide, wide), wide)

    def kv_cols(o):
        return pl.ds(pl.multiple_of(peer(o) * hd, hd), hd)

    small = [
        pltpu.make_async_copy(src, dst, load_sem.at[i])
        for i, (src, dst) in enumerate(
            ((len_hbm, len_ref), (wk_hbm, wk_buf.at[0]), (wq_hbm, wq_buf.at[0]))
        )
    ]
    k_load = [
        pltpu.make_async_copy(k_hbm.at[:, kv_cols(o)], xk.at[o], load_sem.at[4 + o])
        for o in range(n_head)
    ]
    v_load = pltpu.make_async_copy(v_hbm.at[:, kv_cols(0)], v_buf.at[own, :], load_sem.at[3])
    q_load = [
        pltpu.make_async_copy(q_hbm.at[:, q_cols(o)], xq.at[o], load_sem.at[4 + n_head + o])
        for o in range(n_head)
    ]
    @pl.when(me == 0)
    def _():
        for c in (*small, *k_load, v_load, *q_load):
            c.start()

    @pl.when(me != 0)
    def _():
        pl.semaphore_wait(barrier, 1)
        pl.semaphore_signal(here_sem, inc=1, device_id=(b, 0), device_id_type=MESH)

    @pl.when(me == 0)
    def _():
        for c in small:
            c.wait()
        pl.semaphore_wait(here_sem, n_head - 1)

    if n_head > 2:

        @pl.when(me == 0)
        def _():
            for o in others:
                pl.semaphore_signal(all_sem, inc=1, device_id=(b, o), device_id_type=MESH)

        @pl.when(me != 0)
        def _():
            pl.semaphore_wait(all_sem, 1)

    def remote(src, dst, send, recv, o):
        return pltpu.make_async_remote_copy(
            src_ref=src, dst_ref=dst, send_sem=send, recv_sem=recv,
            device_id=(b, peer(o)), device_id_type=MESH,
        )

    def w_copy(o, which, loaded=False):
        slot = n_head - o
        src, dst = (
            (wk_buf.at[0] if loaded else wk_hbm, wk_buf.at[slot]),
            (
                (wq_buf.at[0] if loaded else wq_hbm).at[pair_heads(0)],
                wq_buf.at[slot, pair_heads(0)],
            ),
        )[which]
        return remote(src, dst, w_send.at[slot - 1, which], w_recv.at[slot - 1, which], o)

    def w_pass(o):
        place = wq_buf.at[o, pair_heads(0)]
        return pltpu.make_async_remote_copy(
            src_ref=place, dst_ref=place, send_sem=f_send.at[o - 1], recv_sem=f_recv.at[o - 1],
            device_id=(b + 1 - 2 * second, me), device_id_type=MESH,
        )

    def v_copy(o):
        slot = n_head - o - 1
        return remote(
            v_hbm.at[:, kv_cols(o)], v_buf.at[own, :], kv_send.at[slot, 0], kv_recv.at[slot, 0], o
        )

    def k_copy(o):
        slot = n_head - o - 1
        return remote(
            uk_out.at[slot], uk_in.at[slot], kv_send.at[slot, 1], kv_recv.at[slot, 1], o
        )

    def q_copy(o, n):
        slot = n_head - o - 1
        return remote(
            uq_out.at[slot, n], uq_in.at[slot, n], q_send.at[slot, n], q_recv.at[slot, n], o
        )

    @pl.when(me == 0)
    def _():
        for o in others:
            w_copy(o, 0, True).start()
            w_copy(o, 1, True).start()

    @pl.when(me != 0)
    def _():
        for o in others:
            w_copy(o, 0).start()
            w_copy(o, 1).start()

    for o in others:
        v_copy(o).start()

    @pl.when(me != 0)
    def _():
        for c in (*small, *k_load, v_load, *q_load):
            c.start()

    @pl.when(me == 0)
    def _():
        def greet(i, _):
            @pl.when(i <= n_to)
            def _():
                pl.semaphore_signal(barrier, inc=1, device_id=(b + i, 0), device_id_type=MESH)

            @pl.when(i <= n_from)
            def _():
                pl.semaphore_signal(barrier, inc=1, device_id=(b - i, 0), device_id_type=MESH)

            return 0

        lax.fori_loop(1, reach + 1, greet, 0)

    @pl.when(me != 0)
    def _():
        for c in small:
            c.wait()

    docs = len_ref.shape[1]
    lens = jnp.broadcast_to(len_ref[...].astype(F32), (docs, docs))
    starts = jnp.sum(
        jnp.where(iota((docs, docs), 1) < iota((docs, docs), 0), lens, 0.0), 1, keepdims=True
    )

    def doc_start(pos):
        return jnp.max(jnp.where(starts <= pos, starts, -1.0), 0, keepdims=True)

    lane = iota((1, BLOCK), 1)
    for c in range(blocks):
        pos = (begin + c * BLOCK + lane).astype(F32)
        lo_ref[c] = jnp.broadcast_to(doc_start(pos), (8, BLOCK))
    v_ext[:, hd:, :] = jnp.ones((blocks, ZROWS, BLOCK), BF16)

    def pair_weights(o, p):
        zero = jnp.zeros((half, hd), BF16)
        return jnp.concatenate(
            [
                jnp.concatenate([wq_buf[o, 2 * p], zero], 1),
                jnp.concatenate([zero, wq_buf[o, 2 * p + 1]], 1),
            ],
            0,
        )

    def project(o, p, w, i):
        cols = pl.ds(pl.multiple_of(2 * p * hd, 2 * hd), 2 * hd)
        x = xq[o, token_rows(i * step, step), cols]
        return lax.dot_general(w, x, NT, preferred_element_type=F32)

    def edge_at(pos):
        return doc_start(pos.astype(F32))

    def set_values(c):
        v_ext[c, :hd, :] = v_buf[token_rows(c), :].T

    def set_keys(c, phi):
        keys = phi.astype(BF16).T
        phi_k[c] = keys
        c0 = begin + c * BLOCK
        chosen = ((c0 + lane).astype(F32) >= edge_at(c0 + BLOCK - 1)).astype(F32).astype(BF16)
        fresh[c] = jnp.dot(v_ext[c] * chosen, keys, preferred_element_type=F32)

    k_load[0].wait()
    v_load.wait()

    def own_keys(i, _):
        p = lax.dot_general(
            wk_buf[0], xk[0, token_rows(i * step, step), :], NT, preferred_element_type=F32
        )
        phi = features(p)
        for j in range(step):
            set_values(me * per + i * step + j)
            set_keys(me * per + i * step + j, phi[:, j * BLOCK : (j + 1) * BLOCK])
        return 0

    lax.fori_loop(0, per // step, own_keys, 0, unroll=True)
    q_load[0].wait()
    weights = [pair_weights(0, p) for p in range(2)]

    def own_queries(i, _):
        for p, w in enumerate(weights):
            projected = project(0, p, w, i)
            for m in range(2):
                phi = features(projected[m * half : (m + 1) * half]).astype(BF16)
                for j in range(step):
                    phi_q[i * step + j, p, :, m * hd : (m + 1) * hd] = phi[
                        :, j * BLOCK : (j + 1) * BLOCK
                    ]
        return 0

    lax.fori_loop(0, per // step, own_queries, 0, unroll=True)

    for o in others:
        w_copy(n_head - o, 0).wait_recv()
        k_load[o].wait()
        p = lax.dot_general(wk_buf[o], xk[o], NT, preferred_element_type=F32)
        uk_out[n_head - o - 1] = encode(p)
        k_copy(o).start()
    def send_queries(o, turn):
        w = pair_weights(o, pair(turn))
        for i in range(per // step):
            projected = project(o, pair(turn), w, i)
            for m in range(2):
                u = encode(projected[m * half : (m + 1) * half])
                for j in range(step):
                    n = turn * per + i * step + j
                    uq_out[n_head - o - 1, n, m * half : (m + 1) * half, :] = u[
                        :, j * BLOCK : (j + 1) * BLOCK
                    ]
            for j in range(step):
                n = turn * per + i * step + j
                if n < hold:
                    q_copy(o, n).start()
                else:

                    @pl.when(second == 0)
                    def _(copy=q_copy(o, n)):
                        copy.start()

    for o in others:
        w_copy(n_head - o, 1).wait_recv()
        q_load[o].wait()
        send_queries(o, 0)

    @pl.when(me == 0)
    def _():
        pl.semaphore_wait(barrier, n_to + n_from)
        for o in others:
            pl.semaphore_signal(ctx_sem, inc=1, device_id=(b, o), device_id_type=MESH)

    @pl.when(me != 0)
    def _():
        pl.semaphore_wait(ctx_sem, 1)

    for o in others:
        w_pass(o).start()
    for o in others:
        w_pass(o).wait_recv()
        send_queries(o, 1)

    within = [edge_at(begin + (c + 1) * BLOCK - 1) < (begin + c * BLOCK).astype(F32) for c in range(blocks)]
    across = [edge_at(begin + c * BLOCK - 1) < begin.astype(F32) for c in range(blocks)]
    before = edge_at(begin - 1)
    for o in others:
        v_copy(n_head - o).wait_recv()
        for i in range(per):
            set_values(peer(o) * per + i)
    for o in others:
        k_copy(n_head - o).wait_recv()
        phi = decode(uk_in[o - 1])
        for i in range(per):
            set_keys(peer(o) * per + i, phi[:, i * BLOCK : (i + 1) * BLOCK])

    total = jnp.zeros((hd + ZROWS, hd), F32)
    for c in range(blocks):
        carry[c] = total
        total = fresh[c] + jnp.where(within[c], total, 0.0)
    state_out[...] = total.astype(BF16)

    def s_copy(i):
        return pltpu.make_async_remote_copy(
            src_ref=state_out,
            dst_ref=state_in.at[i - 1],
            send_sem=s_send.at[i - 1],
            recv_sem=s_recv.at[i - 1],
            device_id=(b + i, me),
            device_id_type=MESH,
        )

    def push(i, _):
        @pl.when(i <= n_to)
        def _():
            s_copy(i).start()

        return 0

    lax.fori_loop(1, reach + 1, push, 0)

    if hold < units:

        @pl.when(second == 0)
        def _():
            pl.semaphore_signal(turn_sem, inc=1, device_id=(b + 1, me), device_id_type=MESH)

        @pl.when(second == 1)
        def _():
            pl.semaphore_wait(turn_sem, 1)
            for o in others:
                for n in range(hold, units):
                    q_copy(o, n).start()


    def weigh(c, p, q):
        c0 = begin + c * BLOCK
        scores = jnp.dot(phi_k[c], q, preferred_element_type=F32)
        lo = lo_ref[c, 0:1, :]
        s_i = iota((BLOCK, BLOCK), 0)
        mask = (s_i <= iota((BLOCK, BLOCK), 1)) & ((c0 + s_i).astype(F32) >= lo)
        carried = (lo < c0.astype(F32)).astype(F32).astype(BF16)
        for m in range(2):
            cols = slice(m * hd, (m + 1) * hd)
            mixed[c, p, :BLOCK, cols] = jnp.where(mask, scores[:, cols], 0.0).astype(BF16)
        mixed[c, p, BLOCK:, :] = q * jnp.concatenate([carried] * 2, 1)

    def weigh_sent(o, n):
        q_copy(n_head - o, n).wait_recv()
        u = uq_in[o - 1, n]
        q = jnp.concatenate(
            [decode(u[m * half : (m + 1) * half]).astype(BF16) for m in range(2)], 1
        )
        weigh(peer(o) * per + n % per, pair(n // per), q)

    def collect(i, _):
        @pl.when(i <= n_from)
        def _():
            s_copy(i).wait_recv()
            end = ((b - i + 1) * length - 1).astype(F32)
            carry[blocks] += jnp.where(end >= before, state_in[i - 1].astype(F32), 0.0)

        return 0

    def enter():
        carry[blocks] = jnp.zeros((hd + ZROWS, hd), F32)
        lax.fori_loop(1, reach + 1, collect, 0)
        for c in range(blocks):
            held[c] = (carry[c] + jnp.where(across[c], carry[blocks], 0.0)).astype(BF16)

    order = [(o, n) for o in others for n in range(units)]
    for i in range(per):
        for p in range(2):
            weigh(me * per + i, p, phi_q[i, p])
    todo = []
    for at, (o, n) in enumerate(order[:-1]):
        weigh_sent(o, n)
        if n >= per:
            todo.append((o, n - per))
        if at == 1:
            pl.when(early)(enter)
            todo += [(0, i) for i in range(per)]
        now = todo if at == len(order) - 2 else todo[-2:] if at > 1 else []

        @pl.when(early)
        def _(now=tuple(now)):
            for p, i in now:
                finish(peer(p) * per + i, v_ext, held, mixed, out)

        todo = todo[: len(todo) - len(now)]

    for o in others:
        w_copy(o, 0).wait_send()
        w_copy(o, 1).wait_send()
        v_copy(o).wait_send()
        k_copy(o).wait_send()
        w_pass(o).wait_send()
        for n in range(units):
            q_copy(o, n).wait_send()

    def pushed(i, _):
        @pl.when(i <= n_to)
        def _():
            s_copy(i).wait_send()

        return 0

    lax.fori_loop(1, reach + 1, pushed, 0)

    weigh_sent(*order[-1])

    @pl.when(jnp.logical_not(early))
    def _():
        enter()


def last_kernel(n_ctx, n_head, n0, n1, v_ext, held, mixed, made, out_hbm, out, out_sem):
    me, b = lax.axis_index("head"), lax.axis_index("ctx")
    blocks = mixed.shape[0]
    per = blocks // n_head
    early = span(n_ctx, n0, n1, b)[1] <= EARLY
    last = lax.rem(me + n_head - 1, n_head) * per + per - 1

    def write(c, src):
        rows = token_rows(c)
        return pltpu.make_async_copy(src.at[rows], out_hbm.at[rows], out_sem.at[c])

    @pl.when(early)
    def _():
        for c in range(blocks):

            @pl.when(c != last)
            def _(c=c):
                write(c, made).start()

        finish(last, v_ext, held, mixed, out)
        write(last, out).start()

    @pl.when(jnp.logical_not(early))
    def _():
        for c in range(blocks):
            finish(c, v_ext, held, mixed, out)
            write(c, out).start()

    for c in range(blocks):
        write(c, out).wait()


def body(n_ctx, n_head, queries, keys, values, q_feature, k_feature, doc_lengths):
    rows = queries.shape[0]
    heads, hd, half = q_feature.shape
    length = rows * n_head
    tokens = length * n_ctx
    blocks = length // BLOCK
    per = rows // BLOCK
    first = tokens // 2 - length // 2
    n0, n1 = first // length, (first + SECOND) // length
    reach = min(max(n0, n1 - n0, n_ctx - n1), n_ctx - 1)
    hbm = pl.BlockSpec(memory_space=pltpu.HBM)
    vmem = pl.BlockSpec(memory_space=pltpu.VMEM)
    dma, plain = pltpu.SemaphoreType.DMA, pltpu.SemaphoreType.REGULAR
    others = max(n_head - 1, 1)
    operands = (
        queries, keys, values,
        q_feature.transpose(0, 2, 1), k_feature[0].T,
        doc_lengths.reshape(1, -1),
    )
    parts = pl.pallas_call(
        functools.partial(kernel, n_ctx, n_head, n0, n1, reach),
        out_shape=[
            jax.ShapeDtypeStruct((blocks, hd + ZROWS, BLOCK), BF16),
            jax.ShapeDtypeStruct((blocks, hd + ZROWS, 2 * half), BF16),
            jax.ShapeDtypeStruct((blocks, heads // 2, BLOCK + 2 * half, 2 * BLOCK), BF16),
            jax.ShapeDtypeStruct((length, heads * hd), BF16),
        ],
        in_specs=[hbm] * 6,
        out_specs=[vmem] * 4,
        scratch_shapes=[
            pltpu.VMEM((n_head, rows, heads * hd), BF16),
            pltpu.VMEM((n_head, rows, hd), BF16),
            pltpu.VMEM((length, hd), BF16),
            pltpu.VMEM((n_head, heads, half, hd), BF16),
            pltpu.VMEM((n_head, half, hd), BF16),
            pltpu.VMEM((1, doc_lengths.shape[0]), jnp.int32),
            pltpu.VMEM((others, half, rows), BF16),
            pltpu.VMEM((others, 2 * per, 2 * half, BLOCK), BF16),
            pltpu.VMEM((others, half, rows), BF16),
            pltpu.VMEM((others, 2 * per, 2 * half, BLOCK), BF16),
            pltpu.VMEM((blocks, BLOCK, 2 * half), BF16),
            pltpu.VMEM((per, heads // 2, 2 * half, 2 * BLOCK), BF16),
            pltpu.VMEM((blocks + 1, hd + ZROWS, 2 * half), F32),
            pltpu.VMEM((blocks, hd + ZROWS, 2 * half), F32),
            pltpu.VMEM((blocks, 8, BLOCK), F32),
            pltpu.VMEM((hd + ZROWS, 2 * half), BF16),
            pltpu.VMEM((reach, hd + ZROWS, 2 * half), BF16),
            dma((4 + 2 * n_head,)),
            dma((others, 2)),
            dma((others, 2)),
            dma((others,)),
            dma((others,)),
            dma((others, 2)),
            dma((others, 2)),
            dma((others, 2 * per)),
            dma((others, 2 * per)),
            dma((reach,)),
            dma((reach,)),
            plain, plain, plain, plain,
        ],
        compiler_params=pltpu.CompilerParams(
            collective_id=0, has_side_effects=True, vmem_limit_bytes=32 << 20
        ),
    )(*[pltpu.with_memory_space_constraint(a, pltpu.HBM) for a in operands])
    return pl.pallas_call(
        functools.partial(last_kernel, n_ctx, n_head, n0, n1),
        out_shape=jax.ShapeDtypeStruct((length, heads * hd), BF16),
        in_specs=[vmem] * 4,
        out_specs=hbm,
        scratch_shapes=[pltpu.VMEM((length, heads * hd), BF16), dma((blocks,))],
        compiler_params=pltpu.CompilerParams(vmem_limit_bytes=32 << 20),
    )(*parts)


def solution(mesh):
    placed = (
        P(("ctx", "head"), None),
        P(("ctx", "head"), None),
        P(("ctx", "head"), None),
        P("head", None, None),
        P("head", None, None),
        P(),
    )
    return jax.shard_map(
        functools.partial(body, mesh.shape["ctx"], mesh.shape["head"]),
        mesh=mesh,
        in_specs=placed,
        out_specs=P("ctx", "head"),
        check_vma=False,
    )
```

```python
import functools

import jax
import jax.numpy as jnp
from jax import lax
from jax.experimental import pallas as pl
from jax.experimental.pallas import tpu as pltpu
from jax.sharding import PartitionSpec as P

MESH = pl.DeviceIdType.MESH
F32 = jnp.float32
BF16 = jnp.bfloat16
NT = (((1,), (1,)), ((), ()))
SECOND = 3 * 1024
ZROWS = 16
BLOCK = 128
SPAN = 80.0
EARLY = 1


def iota(shape, dim):
    return lax.broadcasted_iota(jnp.int32, shape, dim)


def extremes(p):
    return jnp.max(p, 0, keepdims=True), jnp.min(p, 0, keepdims=True)


def features(p):
    top, low = extremes(p)
    up, down = jnp.exp(p - top), jnp.exp(low - p)
    up = up * (1.0 / jnp.sum(up, 0, keepdims=True))
    down = down * (1.0 / jnp.sum(down, 0, keepdims=True))
    return jnp.concatenate([up, down], 0)


def encode(p):
    top, low = extremes(p)
    reach = jnp.minimum(SPAN, 0.5 * (top - low))
    return jnp.exp(jnp.maximum(p - top + reach, 0.0) + jnp.minimum(p - low - reach, 0.0)).astype(BF16)


def decode(u):
    up = u.astype(F32)
    down = 1.0 / up
    up = up * (1.0 / jnp.sum(up, 0, keepdims=True))
    down = down * (1.0 / jnp.sum(down, 0, keepdims=True))
    return jnp.concatenate([up, down], 0)


def span(n_ctx, n0, n1, b):
    def last_of(j):
        return jnp.where(j < n0, n0 - 1, jnp.where(j < n1, n1 - 1, n_ctx - 1))

    def first_of(j):
        return jnp.where(j < n0, 0, jnp.where(j < n1, n0, n1))

    return jnp.minimum(last_of(b) + 1, n_ctx - 1) - b, jnp.where(b == 0, 0, b - first_of(b - 1))


def token_rows(i, n=1):
    if isinstance(i, int):
        return pl.ds(i * BLOCK, n * BLOCK)
    return pl.ds(pl.multiple_of(i * BLOCK, BLOCK), n * BLOCK)


def finish(c, v_ext, held, mixed, out):
    hd = BLOCK
    left = jnp.concatenate([v_ext[c], held[c]], 1)
    for p in range(mixed.shape[1]):
        acc = jnp.dot(left, mixed[c, p], preferred_element_type=F32)
        done = (acc[:hd] * (1.0 / acc[hd : hd + 1])).astype(BF16)
        for m in range(2):
            h = 2 * p + m
            out[token_rows(c), h * hd : (h + 1) * hd] = done[:, m * hd : (m + 1) * hd].T


def kernel(
    n_ctx, n_head, n0, n1, reach,
    q_hbm, k_hbm, v_hbm, wq_hbm, wk_hbm, len_hbm, v_ext, held, mixed, out,
    xq, xk, v_buf, wq_buf, wk_buf, len_ref,
    uk_out, uq_out, uk_in, uq_in, phi_k, phi_q, carry, fresh, lo_ref, state_out, state_in,
    load_sem, w_send, w_recv, f_send, f_recv, kv_send, kv_recv, q_send, q_recv, s_send, s_recv,
    here_sem, all_sem, ctx_sem, turn_sem,
):
    me, b = lax.axis_index("head"), lax.axis_index("ctx")
    rows, hd = q_hbm.shape[0], BLOCK
    heads = wq_hbm.shape[0]
    half = hd // 2
    wide = heads * hd
    blocks = phi_k.shape[0]
    per = rows // BLOCK
    step = min(2, per)
    units = 2 * per
    hold = units - 3 if per >= 4 else units
    length = blocks * BLOCK
    begin = b * length
    others = range(1, n_head)
    second = lax.rem(b, 2)

    def pair(turn):
        return lax.rem(second + turn, 2)

    def pair_heads(turn):
        return pl.ds(2 * pair(turn), 2)

    def peer(o):
        return lax.rem(me + o, n_head)

    n_to, n_from = span(n_ctx, n0, n1, b)
    early = n_from <= EARLY

    barrier = pltpu.get_barrier_semaphore()

    @pl.when(me == 0)
    def _():
        for o in others:
            pl.semaphore_signal(barrier, inc=1, device_id=(b, o), device_id_type=MESH)

    own = pl.ds(pl.multiple_of(me * rows, rows), rows)

    def q_cols(o):
        return pl.ds(pl.multiple_of(peer(o) * wide, wide), wide)

    def kv_cols(o):
        return pl.ds(pl.multiple_of(peer(o) * hd, hd), hd)

    small = [
        pltpu.make_async_copy(src, dst, load_sem.at[i])
        for i, (src, dst) in enumerate(
            ((len_hbm, len_ref), (wk_hbm, wk_buf.at[0]), (wq_hbm, wq_buf.at[0]))
        )
    ]
    k_load = [
        pltpu.make_async_copy(k_hbm.at[:, kv_cols(o)], xk.at[o], load_sem.at[4 + o])
        for o in range(n_head)
    ]
    v_load = pltpu.make_async_copy(v_hbm.at[:, kv_cols(0)], v_buf.at[own, :], load_sem.at[3])
    q_load = [
        pltpu.make_async_copy(q_hbm.at[:, q_cols(o)], xq.at[o], load_sem.at[4 + n_head + o])
        for o in range(n_head)
    ]
    @pl.when(me == 0)
    def _():
        for c in (*small, *k_load, v_load, *q_load):
            c.start()

    @pl.when(me != 0)
    def _():
        pl.semaphore_wait(barrier, 1)
        pl.semaphore_signal(here_sem, inc=1, device_id=(b, 0), device_id_type=MESH)

    @pl.when(me == 0)
    def _():
        for c in small:
            c.wait()
        pl.semaphore_wait(here_sem, n_head - 1)

    if n_head > 2:

        @pl.when(me == 0)
        def _():
            for o in others:
                pl.semaphore_signal(all_sem, inc=1, device_id=(b, o), device_id_type=MESH)

        @pl.when(me != 0)
        def _():
            pl.semaphore_wait(all_sem, 1)

    def remote(src, dst, send, recv, o):
        return pltpu.make_async_remote_copy(
            src_ref=src, dst_ref=dst, send_sem=send, recv_sem=recv,
            device_id=(b, peer(o)), device_id_type=MESH,
        )

    def w_copy(o, which, loaded=False):
        slot = n_head - o
        src, dst = (
            (wk_buf.at[0] if loaded else wk_hbm, wk_buf.at[slot]),
            (
                (wq_buf.at[0] if loaded else wq_hbm).at[pair_heads(0)],
                wq_buf.at[slot, pair_heads(0)],
            ),
        )[which]
        return remote(src, dst, w_send.at[slot - 1, which], w_recv.at[slot - 1, which], o)

    def w_pass(o):
        place = wq_buf.at[o, pair_heads(0)]
        return pltpu.make_async_remote_copy(
            src_ref=place, dst_ref=place, send_sem=f_send.at[o - 1], recv_sem=f_recv.at[o - 1],
            device_id=(b + 1 - 2 * second, me), device_id_type=MESH,
        )

    def v_copy(o):
        slot = n_head - o - 1
        return remote(
            v_hbm.at[:, kv_cols(o)], v_buf.at[own, :], kv_send.at[slot, 0], kv_recv.at[slot, 0], o
        )

    def k_copy(o):
        slot = n_head - o - 1
        return remote(
            uk_out.at[slot], uk_in.at[slot], kv_send.at[slot, 1], kv_recv.at[slot, 1], o
        )

    def q_copy(o, n):
        slot = n_head - o - 1
        return remote(
            uq_out.at[slot, n], uq_in.at[slot, n], q_send.at[slot, n], q_recv.at[slot, n], o
        )

    @pl.when(me == 0)
    def _():
        for o in others:
            w_copy(o, 0, True).start()
            w_copy(o, 1, True).start()

    @pl.when(me != 0)
    def _():
        for o in others:
            w_copy(o, 0).start()
            w_copy(o, 1).start()

    for o in others:
        v_copy(o).start()

    @pl.when(me != 0)
    def _():
        for c in (*small, *k_load, v_load, *q_load):
            c.start()

    @pl.when(me == 0)
    def _():
        def greet(i, _):
            @pl.when(i <= n_to)
            def _():
                pl.semaphore_signal(barrier, inc=1, device_id=(b + i, 0), device_id_type=MESH)

            @pl.when(i <= n_from)
            def _():
                pl.semaphore_signal(barrier, inc=1, device_id=(b - i, 0), device_id_type=MESH)

            return 0

        lax.fori_loop(1, reach + 1, greet, 0)

    @pl.when(me != 0)
    def _():
        for c in small:
            c.wait()

    docs = len_ref.shape[1]
    lens = jnp.broadcast_to(len_ref[...].astype(F32), (docs, docs))
    starts = jnp.sum(
        jnp.where(iota((docs, docs), 1) < iota((docs, docs), 0), lens, 0.0), 1, keepdims=True
    )

    def doc_start(pos):
        return jnp.max(jnp.where(starts <= pos, starts, -1.0), 0, keepdims=True)

    lane = iota((1, BLOCK), 1)
    for c in range(blocks):
        pos = (begin + c * BLOCK + lane).astype(F32)
        lo_ref[c] = jnp.broadcast_to(doc_start(pos), (8, BLOCK))
    v_ext[:, hd:, :] = jnp.ones((blocks, ZROWS, BLOCK), BF16)

    def pair_weights(o, p):
        zero = jnp.zeros((half, hd), BF16)
        return jnp.concatenate(
            [
                jnp.concatenate([wq_buf[o, 2 * p], zero], 1),
                jnp.concatenate([zero, wq_buf[o, 2 * p + 1]], 1),
            ],
            0,
        )

    def project(o, p, w, i):
        cols = pl.ds(pl.multiple_of(2 * p * hd, 2 * hd), 2 * hd)
        x = xq[o, token_rows(i * step, step), cols]
        return lax.dot_general(w, x, NT, preferred_element_type=F32)

    def edge_at(pos):
        return doc_start(pos.astype(F32))

    def set_values(c):
        v_ext[c, :hd, :] = v_buf[token_rows(c), :].T

    def set_keys(c, phi):
        keys = phi.astype(BF16).T
        phi_k[c] = keys
        c0 = begin + c * BLOCK
        chosen = ((c0 + lane).astype(F32) >= edge_at(c0 + BLOCK - 1)).astype(F32).astype(BF16)
        fresh[c] = jnp.dot(v_ext[c] * chosen, keys, preferred_element_type=F32)

    k_load[0].wait()
    v_load.wait()

    def own_keys(i, _):
        p = lax.dot_general(
            wk_buf[0], xk[0, token_rows(i * step, step), :], NT, preferred_element_type=F32
        )
        phi = features(p)
        for j in range(step):
            set_values(me * per + i * step + j)
            set_keys(me * per + i * step + j, phi[:, j * BLOCK : (j + 1) * BLOCK])
        return 0

    lax.fori_loop(0, per // step, own_keys, 0, unroll=True)
    q_load[0].wait()
    weights = [pair_weights(0, p) for p in range(2)]

    def own_queries(i, _):
        for p, w in enumerate(weights):
            projected = project(0, p, w, i)
            for m in range(2):
                phi = features(projected[m * half : (m + 1) * half]).astype(BF16)
                for j in range(step):
                    phi_q[i * step + j, p, :, m * hd : (m + 1) * hd] = phi[
                        :, j * BLOCK : (j + 1) * BLOCK
                    ]
        return 0

    lax.fori_loop(0, per // step, own_queries, 0, unroll=True)

    for o in others:
        w_copy(n_head - o, 0).wait_recv()
        k_load[o].wait()
        p = lax.dot_general(wk_buf[o], xk[o], NT, preferred_element_type=F32)
        uk_out[n_head - o - 1] = encode(p)
        k_copy(o).start()
    def send_queries(o, turn):
        w = pair_weights(o, pair(turn))
        for i in range(per // step):
            projected = project(o, pair(turn), w, i)
            for m in range(2):
                u = encode(projected[m * half : (m + 1) * half])
                for j in range(step):
                    n = turn * per + i * step + j
                    uq_out[n_head - o - 1, n, m * half : (m + 1) * half, :] = u[
                        :, j * BLOCK : (j + 1) * BLOCK
                    ]
            for j in range(step):
                n = turn * per + i * step + j
                if n < hold:
                    q_copy(o, n).start()
                else:

                    @pl.when(second == 0)
                    def _(copy=q_copy(o, n)):
                        copy.start()

    for o in others:
        w_copy(n_head - o, 1).wait_recv()
        q_load[o].wait()
        send_queries(o, 0)

    @pl.when(me == 0)
    def _():
        pl.semaphore_wait(barrier, n_to + n_from)
        for o in others:
            pl.semaphore_signal(ctx_sem, inc=1, device_id=(b, o), device_id_type=MESH)

    @pl.when(me != 0)
    def _():
        pl.semaphore_wait(ctx_sem, 1)

    for o in others:
        w_pass(o).start()
    for o in others:
        w_pass(o).wait_recv()
        send_queries(o, 1)

    within = [edge_at(begin + (c + 1) * BLOCK - 1) < (begin + c * BLOCK).astype(F32) for c in range(blocks)]
    across = [edge_at(begin + c * BLOCK - 1) < begin.astype(F32) for c in range(blocks)]
    before = edge_at(begin - 1)
    for o in others:
        v_copy(n_head - o).wait_recv()
        for i in range(per):
            set_values(peer(o) * per + i)
    for o in others:
        k_copy(n_head - o).wait_recv()
        if hold < units and o == 1:

            @pl.when(second == 0)
            def _():
                pl.semaphore_signal(turn_sem, inc=1, device_id=(b + 1, me), device_id_type=MESH)

        phi = decode(uk_in[o - 1])
        for i in range(per):
            set_keys(peer(o) * per + i, phi[:, i * BLOCK : (i + 1) * BLOCK])

    total = jnp.zeros((hd + ZROWS, hd), F32)
    for c in range(blocks):
        carry[c] = total
        total = fresh[c] + jnp.where(within[c], total, 0.0)
    state_out[...] = total.astype(BF16)

    def s_copy(i):
        return pltpu.make_async_remote_copy(
            src_ref=state_out,
            dst_ref=state_in.at[i - 1],
            send_sem=s_send.at[i - 1],
            recv_sem=s_recv.at[i - 1],
            device_id=(b + i, me),
            device_id_type=MESH,
        )

    def push(i, _):
        @pl.when(i <= n_to)
        def _():
            s_copy(i).start()

        return 0

    lax.fori_loop(1, reach + 1, push, 0)

    if hold < units:

        @pl.when(second == 1)
        def _():
            pl.semaphore_wait(turn_sem, 1)
            for o in others:
                for n in range(hold, units):
                    q_copy(o, n).start()


    def weigh(c, p, q):
        c0 = begin + c * BLOCK
        scores = jnp.dot(phi_k[c], q, preferred_element_type=F32)
        lo = lo_ref[c, 0:1, :]
        s_i = iota((BLOCK, BLOCK), 0)
        mask = (s_i <= iota((BLOCK, BLOCK), 1)) & ((c0 + s_i).astype(F32) >= lo)
        carried = (lo < c0.astype(F32)).astype(F32).astype(BF16)
        for m in range(2):
            cols = slice(m * hd, (m + 1) * hd)
            mixed[c, p, :BLOCK, cols] = jnp.where(mask, scores[:, cols], 0.0).astype(BF16)
        mixed[c, p, BLOCK:, :] = q * jnp.concatenate([carried] * 2, 1)

    def weigh_sent(o, n):
        q_copy(n_head - o, n).wait_recv()
        u = uq_in[o - 1, n]
        q = jnp.concatenate(
            [decode(u[m * half : (m + 1) * half]).astype(BF16) for m in range(2)], 1
        )
        weigh(peer(o) * per + n % per, pair(n // per), q)

    def collect(i, _):
        @pl.when(i <= n_from)
        def _():
            s_copy(i).wait_recv()
            end = ((b - i + 1) * length - 1).astype(F32)
            carry[blocks] += jnp.where(end >= before, state_in[i - 1].astype(F32), 0.0)

        return 0

    def enter():
        carry[blocks] = jnp.zeros((hd + ZROWS, hd), F32)
        lax.fori_loop(1, reach + 1, collect, 0)
        for c in range(blocks):
            held[c] = (carry[c] + jnp.where(across[c], carry[blocks], 0.0)).astype(BF16)

    order = [(o, n) for o in others for n in range(units)]
    for i in range(per):
        for p in range(2):
            weigh(me * per + i, p, phi_q[i, p])
    todo = []
    for at, (o, n) in enumerate(order[:-1]):
        weigh_sent(o, n)
        if n >= per:
            todo.append((o, n - per))
        if at == 1:
            pl.when(early)(enter)
            todo += [(0, i) for i in range(per)]
        now = todo if at == len(order) - 2 else todo[-2:] if at > 1 else []

        @pl.when(early)
        def _(now=tuple(now)):
            for p, i in now:
                finish(peer(p) * per + i, v_ext, held, mixed, out)

        todo = todo[: len(todo) - len(now)]

    for o in others:
        w_copy(o, 0).wait_send()
        w_copy(o, 1).wait_send()
        v_copy(o).wait_send()
        k_copy(o).wait_send()
        w_pass(o).wait_send()
        for n in range(units):
            q_copy(o, n).wait_send()

    def pushed(i, _):
        @pl.when(i <= n_to)
        def _():
            s_copy(i).wait_send()

        return 0

    lax.fori_loop(1, reach + 1, pushed, 0)

    weigh_sent(*order[-1])

    @pl.when(jnp.logical_not(early))
    def _():
        enter()


def last_kernel(n_ctx, n_head, n0, n1, v_ext, held, mixed, made, out_hbm, out, out_sem):
    me, b = lax.axis_index("head"), lax.axis_index("ctx")
    blocks = mixed.shape[0]
    per = blocks // n_head
    early = span(n_ctx, n0, n1, b)[1] <= EARLY
    last = lax.rem(me + n_head - 1, n_head) * per + per - 1

    def write(c, src):
        rows = token_rows(c)
        return pltpu.make_async_copy(src.at[rows], out_hbm.at[rows], out_sem.at[c])

    @pl.when(early)
    def _():
        for c in range(blocks):

            @pl.when(c != last)
            def _(c=c):
                write(c, made).start()

        finish(last, v_ext, held, mixed, out)
        write(last, out).start()

    @pl.when(jnp.logical_not(early))
    def _():
        for c in range(blocks):
            finish(c, v_ext, held, mixed, out)
            write(c, out).start()

    for c in range(blocks):
        write(c, out).wait()


def body(n_ctx, n_head, queries, keys, values, q_feature, k_feature, doc_lengths):
    rows = queries.shape[0]
    heads, hd, half = q_feature.shape
    length = rows * n_head
    tokens = length * n_ctx
    blocks = length // BLOCK
    per = rows // BLOCK
    first = tokens // 2 - length // 2
    n0, n1 = first // length, (first + SECOND) // length
    reach = min(max(n0, n1 - n0, n_ctx - n1), n_ctx - 1)
    hbm = pl.BlockSpec(memory_space=pltpu.HBM)
    vmem = pl.BlockSpec(memory_space=pltpu.VMEM)
    dma, plain = pltpu.SemaphoreType.DMA, pltpu.SemaphoreType.REGULAR
    others = max(n_head - 1, 1)
    operands = (
        queries, keys, values,
        q_feature.transpose(0, 2, 1), k_feature[0].T,
        doc_lengths.reshape(1, -1),
    )
    parts = pl.pallas_call(
        functools.partial(kernel, n_ctx, n_head, n0, n1, reach),
        out_shape=[
            jax.ShapeDtypeStruct((blocks, hd + ZROWS, BLOCK), BF16),
            jax.ShapeDtypeStruct((blocks, hd + ZROWS, 2 * half), BF16),
            jax.ShapeDtypeStruct((blocks, heads // 2, BLOCK + 2 * half, 2 * BLOCK), BF16),
            jax.ShapeDtypeStruct((length, heads * hd), BF16),
        ],
        in_specs=[hbm] * 6,
        out_specs=[vmem] * 4,
        scratch_shapes=[
            pltpu.VMEM((n_head, rows, heads * hd), BF16),
            pltpu.VMEM((n_head, rows, hd), BF16),
            pltpu.VMEM((length, hd), BF16),
            pltpu.VMEM((n_head, heads, half, hd), BF16),
            pltpu.VMEM((n_head, half, hd), BF16),
            pltpu.VMEM((1, doc_lengths.shape[0]), jnp.int32),
            pltpu.VMEM((others, half, rows), BF16),
            pltpu.VMEM((others, 2 * per, 2 * half, BLOCK), BF16),
            pltpu.VMEM((others, half, rows), BF16),
            pltpu.VMEM((others, 2 * per, 2 * half, BLOCK), BF16),
            pltpu.VMEM((blocks, BLOCK, 2 * half), BF16),
            pltpu.VMEM((per, heads // 2, 2 * half, 2 * BLOCK), BF16),
            pltpu.VMEM((blocks + 1, hd + ZROWS, 2 * half), F32),
            pltpu.VMEM((blocks, hd + ZROWS, 2 * half), F32),
            pltpu.VMEM((blocks, 8, BLOCK), F32),
            pltpu.VMEM((hd + ZROWS, 2 * half), BF16),
            pltpu.VMEM((reach, hd + ZROWS, 2 * half), BF16),
            dma((4 + 2 * n_head,)),
            dma((others, 2)),
            dma((others, 2)),
            dma((others,)),
            dma((others,)),
            dma((others, 2)),
            dma((others, 2)),
            dma((others, 2 * per)),
            dma((others, 2 * per)),
            dma((reach,)),
            dma((reach,)),
            plain, plain, plain, plain,
        ],
        compiler_params=pltpu.CompilerParams(
            collective_id=0, has_side_effects=True, vmem_limit_bytes=32 << 20
        ),
    )(*[pltpu.with_memory_space_constraint(a, pltpu.HBM) for a in operands])
    return pl.pallas_call(
        functools.partial(last_kernel, n_ctx, n_head, n0, n1),
        out_shape=jax.ShapeDtypeStruct((length, heads * hd), BF16),
        in_specs=[vmem] * 4,
        out_specs=hbm,
        scratch_shapes=[pltpu.VMEM((length, heads * hd), BF16), dma((blocks,))],
        compiler_params=pltpu.CompilerParams(vmem_limit_bytes=32 << 20),
    )(*parts)


def solution(mesh):
    placed = (
        P(("ctx", "head"), None),
        P(("ctx", "head"), None),
        P(("ctx", "head"), None),
        P("head", None, None),
        P("head", None, None),
        P(),
    )
    return jax.shard_map(
        functools.partial(body, mesh.shape["ctx"], mesh.shape["head"]),
        mesh=mesh,
        in_specs=placed,
        out_specs=P("ctx", "head"),
        check_vma=False,
    )
```

```python
import functools

import jax
import jax.numpy as jnp
from jax import lax
from jax.experimental import pallas as pl
from jax.experimental.pallas import tpu as pltpu
from jax.sharding import PartitionSpec as P

MESH = pl.DeviceIdType.MESH
F32 = jnp.float32
BF16 = jnp.bfloat16
NT = (((1,), (1,)), ((), ()))
SECOND = 3 * 1024
ZROWS = 16
BLOCK = 128
SPAN = 80.0
EARLY = 3


def iota(shape, dim):
    return lax.broadcasted_iota(jnp.int32, shape, dim)


def extremes(p):
    return jnp.max(p, 0, keepdims=True), jnp.min(p, 0, keepdims=True)


def features(p):
    top, low = extremes(p)
    up, down = jnp.exp(p - top), jnp.exp(low - p)
    up = up * (1.0 / jnp.sum(up, 0, keepdims=True))
    down = down * (1.0 / jnp.sum(down, 0, keepdims=True))
    return jnp.concatenate([up, down], 0)


def encode(p):
    top, low = extremes(p)
    reach = jnp.minimum(SPAN, 0.5 * (top - low))
    return jnp.exp(jnp.maximum(p - top + reach, 0.0) + jnp.minimum(p - low - reach, 0.0)).astype(BF16)


def decode(u):
    up = u.astype(F32)
    down = 1.0 / up
    up = up * (1.0 / jnp.sum(up, 0, keepdims=True))
    down = down * (1.0 / jnp.sum(down, 0, keepdims=True))
    return jnp.concatenate([up, down], 0)


def span(n_ctx, n0, n1, b):
    def last_of(j):
        return jnp.where(j < n0, n0 - 1, jnp.where(j < n1, n1 - 1, n_ctx - 1))

    def first_of(j):
        return jnp.where(j < n0, 0, jnp.where(j < n1, n0, n1))

    return jnp.minimum(last_of(b) + 1, n_ctx - 1) - b, jnp.where(b == 0, 0, b - first_of(b - 1))


def token_rows(i, n=1):
    if isinstance(i, int):
        return pl.ds(i * BLOCK, n * BLOCK)
    return pl.ds(pl.multiple_of(i * BLOCK, BLOCK), n * BLOCK)


def finish(c, v_ext, held, mixed, out):
    hd = BLOCK
    left = jnp.concatenate([v_ext[c], held[c]], 1)
    for p in range(mixed.shape[1]):
        acc = jnp.dot(left, mixed[c, p], preferred_element_type=F32)
        done = (acc[:hd] * (1.0 / acc[hd : hd + 1])).astype(BF16)
        for m in range(2):
            h = 2 * p + m
            out[token_rows(c), h * hd : (h + 1) * hd] = done[:, m * hd : (m + 1) * hd].T


def kernel(
    n_ctx, n_head, n0, n1, reach,
    q_hbm, k_hbm, v_hbm, wq_hbm, wk_hbm, len_hbm, v_ext, held, mixed, out,
    xq, xk, v_buf, wq_buf, wk_buf, len_ref,
    uk_out, uq_out, uk_in, uq_in, phi_k, phi_q, carry, fresh, lo_ref, state_out, state_in,
    load_sem, w_send, w_recv, f_send, f_recv, kv_send, kv_recv, q_send, q_recv, s_send, s_recv,
    here_sem, all_sem, ctx_sem, turn_sem,
):
    me, b = lax.axis_index("head"), lax.axis_index("ctx")
    rows, hd = q_hbm.shape[0], BLOCK
    heads = wq_hbm.shape[0]
    half = hd // 2
    wide = heads * hd
    blocks = phi_k.shape[0]
    per = rows // BLOCK
    step = min(2, per)
    units = 2 * per
    hold = units - 3 if per >= 4 else units
    length = blocks * BLOCK
    begin = b * length
    others = range(1, n_head)
    second = lax.rem(b, 2)

    def pair(turn):
        return lax.rem(second + turn, 2)

    def pair_heads(turn):
        return pl.ds(2 * pair(turn), 2)

    def peer(o):
        return lax.rem(me + o, n_head)

    n_to, n_from = span(n_ctx, n0, n1, b)
    early = n_from <= EARLY

    barrier = pltpu.get_barrier_semaphore()

    @pl.when(me == 0)
    def _():
        for o in others:
            pl.semaphore_signal(barrier, inc=1, device_id=(b, o), device_id_type=MESH)

    own = pl.ds(pl.multiple_of(me * rows, rows), rows)

    def q_cols(o):
        return pl.ds(pl.multiple_of(peer(o) * wide, wide), wide)

    def kv_cols(o):
        return pl.ds(pl.multiple_of(peer(o) * hd, hd), hd)

    small = [
        pltpu.make_async_copy(src, dst, load_sem.at[i])
        for i, (src, dst) in enumerate(
            ((len_hbm, len_ref), (wk_hbm, wk_buf.at[0]), (wq_hbm, wq_buf.at[0]))
        )
    ]
    k_load = [
        pltpu.make_async_copy(k_hbm.at[:, kv_cols(o)], xk.at[o], load_sem.at[4 + o])
        for o in range(n_head)
    ]
    v_load = pltpu.make_async_copy(v_hbm.at[:, kv_cols(0)], v_buf.at[own, :], load_sem.at[3])
    q_load = [
        pltpu.make_async_copy(q_hbm.at[:, q_cols(o)], xq.at[o], load_sem.at[4 + n_head + o])
        for o in range(n_head)
    ]
    @pl.when(me == 0)
    def _():
        for c in (*small, *k_load, v_load, *q_load):
            c.start()

    @pl.when(me != 0)
    def _():
        pl.semaphore_wait(barrier, 1)
        pl.semaphore_signal(here_sem, inc=1, device_id=(b, 0), device_id_type=MESH)

    @pl.when(me == 0)
    def _():
        for c in small:
            c.wait()
        pl.semaphore_wait(here_sem, n_head - 1)

    if n_head > 2:

        @pl.when(me == 0)
        def _():
            for o in others:
                pl.semaphore_signal(all_sem, inc=1, device_id=(b, o), device_id_type=MESH)

        @pl.when(me != 0)
        def _():
            pl.semaphore_wait(all_sem, 1)

    def remote(src, dst, send, recv, o):
        return pltpu.make_async_remote_copy(
            src_ref=src, dst_ref=dst, send_sem=send, recv_sem=recv,
            device_id=(b, peer(o)), device_id_type=MESH,
        )

    def w_copy(o, which, loaded=False):
        slot = n_head - o
        src, dst = (
            (wk_buf.at[0] if loaded else wk_hbm, wk_buf.at[slot]),
            (
                (wq_buf.at[0] if loaded else wq_hbm).at[pair_heads(0)],
                wq_buf.at[slot, pair_heads(0)],
            ),
        )[which]
        return remote(src, dst, w_send.at[slot - 1, which], w_recv.at[slot - 1, which], o)

    def w_pass(o):
        place = wq_buf.at[o, pair_heads(0)]
        return pltpu.make_async_remote_copy(
            src_ref=place, dst_ref=place, send_sem=f_send.at[o - 1], recv_sem=f_recv.at[o - 1],
            device_id=(b + 1 - 2 * second, me), device_id_type=MESH,
        )

    def v_copy(o):
        slot = n_head - o - 1
        return remote(
            v_hbm.at[:, kv_cols(o)], v_buf.at[own, :], kv_send.at[slot, 0], kv_recv.at[slot, 0], o
        )

    def k_copy(o):
        slot = n_head - o - 1
        return remote(
            uk_out.at[slot], uk_in.at[slot], kv_send.at[slot, 1], kv_recv.at[slot, 1], o
        )

    def q_copy(o, n):
        slot = n_head - o - 1
        return remote(
            uq_out.at[slot, n], uq_in.at[slot, n], q_send.at[slot, n], q_recv.at[slot, n], o
        )

    @pl.when(me == 0)
    def _():
        for o in others:
            w_copy(o, 0, True).start()
            w_copy(o, 1, True).start()

    @pl.when(me != 0)
    def _():
        for o in others:
            w_copy(o, 0).start()
            w_copy(o, 1).start()

    for o in others:
        v_copy(o).start()

    @pl.when(me != 0)
    def _():
        for c in (*small, *k_load, v_load, *q_load):
            c.start()

    @pl.when(me == 0)
    def _():
        def greet(i, _):
            @pl.when(i <= n_to)
            def _():
                pl.semaphore_signal(barrier, inc=1, device_id=(b + i, 0), device_id_type=MESH)

            @pl.when(i <= n_from)
            def _():
                pl.semaphore_signal(barrier, inc=1, device_id=(b - i, 0), device_id_type=MESH)

            return 0

        lax.fori_loop(1, reach + 1, greet, 0)

    @pl.when(me != 0)
    def _():
        for c in small:
            c.wait()

    docs = len_ref.shape[1]
    lens = jnp.broadcast_to(len_ref[...].astype(F32), (docs, docs))
    starts = jnp.sum(
        jnp.where(iota((docs, docs), 1) < iota((docs, docs), 0), lens, 0.0), 1, keepdims=True
    )

    def doc_start(pos):
        return jnp.max(jnp.where(starts <= pos, starts, -1.0), 0, keepdims=True)

    lane = iota((1, BLOCK), 1)
    for c in range(blocks):
        pos = (begin + c * BLOCK + lane).astype(F32)
        lo_ref[c] = jnp.broadcast_to(doc_start(pos), (8, BLOCK))
    v_ext[:, hd:, :] = jnp.ones((blocks, ZROWS, BLOCK), BF16)

    def pair_weights(o, p):
        zero = jnp.zeros((half, hd), BF16)
        return jnp.concatenate(
            [
                jnp.concatenate([wq_buf[o, 2 * p], zero], 1),
                jnp.concatenate([zero, wq_buf[o, 2 * p + 1]], 1),
            ],
            0,
        )

    def project(o, p, w, i):
        cols = pl.ds(pl.multiple_of(2 * p * hd, 2 * hd), 2 * hd)
        x = xq[o, token_rows(i * step, step), cols]
        return lax.dot_general(w, x, NT, preferred_element_type=F32)

    def edge_at(pos):
        return doc_start(pos.astype(F32))

    def set_values(c):
        v_ext[c, :hd, :] = v_buf[token_rows(c), :].T

    def set_keys(c, phi):
        keys = phi.astype(BF16).T
        phi_k[c] = keys
        c0 = begin + c * BLOCK
        chosen = ((c0 + lane).astype(F32) >= edge_at(c0 + BLOCK - 1)).astype(F32).astype(BF16)
        fresh[c] = jnp.dot(v_ext[c] * chosen, keys, preferred_element_type=F32)

    k_load[0].wait()
    v_load.wait()

    def own_keys(i, _):
        p = lax.dot_general(
            wk_buf[0], xk[0, token_rows(i * step, step), :], NT, preferred_element_type=F32
        )
        phi = features(p)
        for j in range(step):
            set_values(me * per + i * step + j)
            set_keys(me * per + i * step + j, phi[:, j * BLOCK : (j + 1) * BLOCK])
        return 0

    lax.fori_loop(0, per // step, own_keys, 0, unroll=True)
    q_load[0].wait()
    weights = [pair_weights(0, p) for p in range(2)]

    def own_queries(i, _):
        for p, w in enumerate(weights):
            projected = project(0, p, w, i)
            for m in range(2):
                phi = features(projected[m * half : (m + 1) * half]).astype(BF16)
                for j in range(step):
                    phi_q[i * step + j, p, :, m * hd : (m + 1) * hd] = phi[
                        :, j * BLOCK : (j + 1) * BLOCK
                    ]
        return 0

    lax.fori_loop(0, per // step, own_queries, 0, unroll=True)

    for o in others:
        w_copy(n_head - o, 0).wait_recv()
        k_load[o].wait()
        p = lax.dot_general(wk_buf[o], xk[o], NT, preferred_element_type=F32)
        uk_out[n_head - o - 1] = encode(p)
        k_copy(o).start()
    def send_queries(o, turn):
        w = pair_weights(o, pair(turn))
        for i in range(per // step):
            projected = project(o, pair(turn), w, i)
            for m in range(2):
                u = encode(projected[m * half : (m + 1) * half])
                for j in range(step):
                    n = turn * per + i * step + j
                    uq_out[n_head - o - 1, n, m * half : (m + 1) * half, :] = u[
                        :, j * BLOCK : (j + 1) * BLOCK
                    ]
            for j in range(step):
                n = turn * per + i * step + j
                if n < hold:
                    q_copy(o, n).start()
                else:

                    @pl.when(second == 0)
                    def _(copy=q_copy(o, n)):
                        copy.start()

    for o in others:
        w_copy(n_head - o, 1).wait_recv()
        q_load[o].wait()
        send_queries(o, 0)

    @pl.when(me == 0)
    def _():
        pl.semaphore_wait(barrier, n_to + n_from)
        for o in others:
            pl.semaphore_signal(ctx_sem, inc=1, device_id=(b, o), device_id_type=MESH)

    @pl.when(me != 0)
    def _():
        pl.semaphore_wait(ctx_sem, 1)

    for o in others:
        w_pass(o).start()
    for o in others:
        w_pass(o).wait_recv()
        send_queries(o, 1)

    within = [edge_at(begin + (c + 1) * BLOCK - 1) < (begin + c * BLOCK).astype(F32) for c in range(blocks)]
    across = [edge_at(begin + c * BLOCK - 1) < begin.astype(F32) for c in range(blocks)]
    before = edge_at(begin - 1)
    for o in others:
        v_copy(n_head - o).wait_recv()
        for i in range(per):
            set_values(peer(o) * per + i)
    for o in others:
        k_copy(n_head - o).wait_recv()
        phi = decode(uk_in[o - 1])
        for i in range(per):
            set_keys(peer(o) * per + i, phi[:, i * BLOCK : (i + 1) * BLOCK])

    total = jnp.zeros((hd + ZROWS, hd), F32)
    for c in range(blocks):
        carry[c] = total
        total = fresh[c] + jnp.where(within[c], total, 0.0)
    state_out[...] = total.astype(BF16)

    def s_copy(i):
        return pltpu.make_async_remote_copy(
            src_ref=state_out,
            dst_ref=state_in.at[i - 1],
            send_sem=s_send.at[i - 1],
            recv_sem=s_recv.at[i - 1],
            device_id=(b + i, me),
            device_id_type=MESH,
        )

    def push(i, _):
        @pl.when(i <= n_to)
        def _():
            s_copy(i).start()

        return 0

    lax.fori_loop(1, reach + 1, push, 0)

    if hold < units:

        @pl.when(second == 0)
        def _():
            pl.semaphore_signal(turn_sem, inc=1, device_id=(b + 1, me), device_id_type=MESH)

        @pl.when(second == 1)
        def _():
            pl.semaphore_wait(turn_sem, 1)
            for o in others:
                for n in range(hold, units):
                    q_copy(o, n).start()


    def weigh(c, p, q):
        c0 = begin + c * BLOCK
        scores = jnp.dot(phi_k[c], q, preferred_element_type=F32)
        lo = lo_ref[c, 0:1, :]
        s_i = iota((BLOCK, BLOCK), 0)
        mask = (s_i <= iota((BLOCK, BLOCK), 1)) & ((c0 + s_i).astype(F32) >= lo)
        carried = (lo < c0.astype(F32)).astype(F32).astype(BF16)
        for m in range(2):
            cols = slice(m * hd, (m + 1) * hd)
            mixed[c, p, :BLOCK, cols] = jnp.where(mask, scores[:, cols], 0.0).astype(BF16)
        mixed[c, p, BLOCK:, :] = q * jnp.concatenate([carried] * 2, 1)

    def weigh_sent(o, n):
        q_copy(n_head - o, n).wait_recv()
        u = uq_in[o - 1, n]
        q = jnp.concatenate(
            [decode(u[m * half : (m + 1) * half]).astype(BF16) for m in range(2)], 1
        )
        weigh(peer(o) * per + n % per, pair(n // per), q)

    def collect(i, _):
        @pl.when(i <= n_from)
        def _():
            s_copy(i).wait_recv()
            end = ((b - i + 1) * length - 1).astype(F32)
            carry[blocks] += jnp.where(end >= before, state_in[i - 1].astype(F32), 0.0)

        return 0

    def enter():
        carry[blocks] = jnp.zeros((hd + ZROWS, hd), F32)
        lax.fori_loop(1, reach + 1, collect, 0)
        for c in range(blocks):
            held[c] = (carry[c] + jnp.where(across[c], carry[blocks], 0.0)).astype(BF16)

    order = [(o, n) for o in others for n in range(units)]
    for i in range(per):
        for p in range(2):
            weigh(me * per + i, p, phi_q[i, p])
    todo = []
    for at, (o, n) in enumerate(order[:-1]):
        weigh_sent(o, n)
        if n >= per:
            todo.append((o, n - per))
        if at == 1:
            pl.when(n_from <= 1)(enter)
            todo += [(0, i) for i in range(per)]
        now = todo if at == len(order) - 2 else todo[-2:] if at > 1 else []

        @pl.when(n_from <= 1)
        def _(now=tuple(now)):
            for p, i in now:
                finish(peer(p) * per + i, v_ext, held, mixed, out)

        todo = todo[: len(todo) - len(now)]

    @pl.when(early & (n_from > 1))
    def _():
        enter()
        for p, i in [(p, i) for p in range(n_head) for i in range(per)][:-1]:
            finish(peer(p) * per + i, v_ext, held, mixed, out)

    for o in others:
        w_copy(o, 0).wait_send()
        w_copy(o, 1).wait_send()
        v_copy(o).wait_send()
        k_copy(o).wait_send()
        w_pass(o).wait_send()
        for n in range(units):
            q_copy(o, n).wait_send()

    def pushed(i, _):
        @pl.when(i <= n_to)
        def _():
            s_copy(i).wait_send()

        return 0

    lax.fori_loop(1, reach + 1, pushed, 0)

    weigh_sent(*order[-1])

    @pl.when(jnp.logical_not(early))
    def _():
        enter()


def last_kernel(n_ctx, n_head, n0, n1, v_ext, held, mixed, made, out_hbm, out, out_sem):
    me, b = lax.axis_index("head"), lax.axis_index("ctx")
    blocks = mixed.shape[0]
    per = blocks // n_head
    early = span(n_ctx, n0, n1, b)[1] <= EARLY
    last = lax.rem(me + n_head - 1, n_head) * per + per - 1

    def write(c, src):
        rows = token_rows(c)
        return pltpu.make_async_copy(src.at[rows], out_hbm.at[rows], out_sem.at[c])

    @pl.when(early)
    def _():
        for c in range(blocks):

            @pl.when(c != last)
            def _(c=c):
                write(c, made).start()

        finish(last, v_ext, held, mixed, out)
        write(last, out).start()

    @pl.when(jnp.logical_not(early))
    def _():
        for c in range(blocks):
            finish(c, v_ext, held, mixed, out)
            write(c, out).start()

    for c in range(blocks):
        write(c, out).wait()


def body(n_ctx, n_head, queries, keys, values, q_feature, k_feature, doc_lengths):
    rows = queries.shape[0]
    heads, hd, half = q_feature.shape
    length = rows * n_head
    tokens = length * n_ctx
    blocks = length // BLOCK
    per = rows // BLOCK
    first = tokens // 2 - length // 2
    n0, n1 = first // length, (first + SECOND) // length
    reach = min(max(n0, n1 - n0, n_ctx - n1), n_ctx - 1)
    hbm = pl.BlockSpec(memory_space=pltpu.HBM)
    vmem = pl.BlockSpec(memory_space=pltpu.VMEM)
    dma, plain = pltpu.SemaphoreType.DMA, pltpu.SemaphoreType.REGULAR
    others = max(n_head - 1, 1)
    operands = (
        queries, keys, values,
        q_feature.transpose(0, 2, 1), k_feature[0].T,
        doc_lengths.reshape(1, -1),
    )
    parts = pl.pallas_call(
        functools.partial(kernel, n_ctx, n_head, n0, n1, reach),
        out_shape=[
            jax.ShapeDtypeStruct((blocks, hd + ZROWS, BLOCK), BF16),
            jax.ShapeDtypeStruct((blocks, hd + ZROWS, 2 * half), BF16),
            jax.ShapeDtypeStruct((blocks, heads // 2, BLOCK + 2 * half, 2 * BLOCK), BF16),
            jax.ShapeDtypeStruct((length, heads * hd), BF16),
        ],
        in_specs=[hbm] * 6,
        out_specs=[vmem] * 4,
        scratch_shapes=[
            pltpu.VMEM((n_head, rows, heads * hd), BF16),
            pltpu.VMEM((n_head, rows, hd), BF16),
            pltpu.VMEM((length, hd), BF16),
            pltpu.VMEM((n_head, heads, half, hd), BF16),
            pltpu.VMEM((n_head, half, hd), BF16),
            pltpu.VMEM((1, doc_lengths.shape[0]), jnp.int32),
            pltpu.VMEM((others, half, rows), BF16),
            pltpu.VMEM((others, 2 * per, 2 * half, BLOCK), BF16),
            pltpu.VMEM((others, half, rows), BF16),
            pltpu.VMEM((others, 2 * per, 2 * half, BLOCK), BF16),
            pltpu.VMEM((blocks, BLOCK, 2 * half), BF16),
            pltpu.VMEM((per, heads // 2, 2 * half, 2 * BLOCK), BF16),
            pltpu.VMEM((blocks + 1, hd + ZROWS, 2 * half), F32),
            pltpu.VMEM((blocks, hd + ZROWS, 2 * half), F32),
            pltpu.VMEM((blocks, 8, BLOCK), F32),
            pltpu.VMEM((hd + ZROWS, 2 * half), BF16),
            pltpu.VMEM((reach, hd + ZROWS, 2 * half), BF16),
            dma((4 + 2 * n_head,)),
            dma((others, 2)),
            dma((others, 2)),
            dma((others,)),
            dma((others,)),
            dma((others, 2)),
            dma((others, 2)),
            dma((others, 2 * per)),
            dma((others, 2 * per)),
            dma((reach,)),
            dma((reach,)),
            plain, plain, plain, plain,
        ],
        compiler_params=pltpu.CompilerParams(
            collective_id=0, has_side_effects=True, vmem_limit_bytes=32 << 20
        ),
    )(*[pltpu.with_memory_space_constraint(a, pltpu.HBM) for a in operands])
    return pl.pallas_call(
        functools.partial(last_kernel, n_ctx, n_head, n0, n1),
        out_shape=jax.ShapeDtypeStruct((length, heads * hd), BF16),
        in_specs=[vmem] * 4,
        out_specs=hbm,
        scratch_shapes=[pltpu.VMEM((length, heads * hd), BF16), dma((blocks,))],
        compiler_params=pltpu.CompilerParams(vmem_limit_bytes=32 << 20),
    )(*parts)


def solution(mesh):
    placed = (
        P(("ctx", "head"), None),
        P(("ctx", "head"), None),
        P(("ctx", "head"), None),
        P("head", None, None),
        P("head", None, None),
        P(),
    )
    return jax.shard_map(
        functools.partial(body, mesh.shape["ctx"], mesh.shape["head"]),
        mesh=mesh,
        in_specs=placed,
        out_specs=P("ctx", "head"),
        check_vma=False,
    )
```
